256 devices in a mesh: seq: 64 (over z, y, core), head: 4 (over x).
Axes of the slice: x: 4, y: 4, z: 8, core: 2. Of those that a mesh axis runs over, the one named last changes fastest.
Arguments:
- queries: bfloat16 [32768, 2048], P('seq', 'head'), may hold values from -8 to 8
- keys: bfloat16 [32768, 1024], P('seq', 'head'), may hold values from -8 to 8
- values: bfloat16 [32768, 1024], P('seq', 'head'), may hold values from -6 to 6
- output_gradient: bfloat16 [32768, 2048], P('seq', 'head'), may hold values from -6 to 6
- key_exponents: int32 [256, 8], P('seq', 'head'), may hold values from -1 to 1
- value_exponents: int32 [256, 8], P('seq', 'head'), may hold values from -1 to 1
- key_matrix: bfloat16 [5376, 1024], P(None, 'head'), may hold values from -0.1875 to 0.1875
- value_matrix: bfloat16 [5376, 1024], P(None, 'head'), may hold values from -0.1875 to 0.1875
Outputs:
- query_grad: bfloat16 [32768, 2048], P('seq', 'head')
- input_grad: bfloat16 [5376, 32768], P('head', 'seq')
The draws below stay inside these ranges and needn't reach their ends.
All inputs are finite; a program needn't handle non-finite values.
Results may differ from the reference program's by a relative error of at most 0.015.
Values may be sent and summed in bfloat16 or wider, within the bound.
No kernel may reach another device: no remote copies, remote signals or barrier semaphores. Data moves between devices by JAX's collectives and lax.ppermute only.
A program may use at most 64 MiB of HBM per device.

```python
import math
import jax
import jax.numpy as jnp
from jax import lax

MODEL_WIDTH = 5376
QUERY_HEADS = 16
KEY_VALUE_HEADS = 8
HEAD_SIZE = 128
QUERY_SCALE = 168
ATTEND_WINDOW = 1024
SCALE_BLOCK = 128
SEQUENCE_TOKENS = 32768
N_HEAD = 4


def draw_queries(key, part):
    window_entries = jax.random.normal(jax.random.fold_in(key, 5), (SEQUENCE_TOKENS, QUERY_HEADS, HEAD_SIZE), jnp.float32)
    return jnp.clip(window_entries, -8.0, 8.0).reshape(SEQUENCE_TOKENS, QUERY_HEADS * HEAD_SIZE).astype(jnp.bfloat16)


def draw_keys(key, part):
    window_offsets = jax.random.normal(jax.random.fold_in(key, 7), (SEQUENCE_TOKENS // SCALE_BLOCK, KEY_VALUE_HEADS, HEAD_SIZE), jnp.float32)
    window_offsets = jnp.repeat(window_offsets, SCALE_BLOCK, axis=0)
    window_entries = jax.random.normal(jax.random.fold_in(key, 6), (SEQUENCE_TOKENS, KEY_VALUE_HEADS, HEAD_SIZE), jnp.float32) + window_offsets
    return jnp.clip(window_entries, -8.0, 8.0).reshape(SEQUENCE_TOKENS, KEY_VALUE_HEADS * HEAD_SIZE).astype(jnp.bfloat16)


def place_ends(values, stream_key, low, top_value):
    longest = values.shape.index(max(values.shape))
    spots = []
    for shift in (0, 1):
        where = [jax.random.randint(jax.random.fold_in(stream_key, axis), (), 0, length) for axis, length in enumerate(values.shape)]
        where[longest] = (where[longest] + shift) % values.shape[longest]
        spots.append(tuple(where))
    return values.at[spots[0]].set(low).at[spots[1]].set(top_value)


def level_of(key, dims, shards, low, top_value):
    def one(axis_at, shards_of):
        heights = jax.random.uniform(jax.random.fold_in(jax.random.fold_in(key, 6), axis_at), (shards_of,), jnp.float32, low / len(shards), top_value / len(shards))
        return jnp.repeat(jnp.exp(heights), dims[axis_at] // shards_of).reshape((-1,) + (1,) * (len(dims) - axis_at - 1))

    gain = one(*shards[0])
    for cut in shards[1:]:
        gain = gain * one(*cut)
    return gain


def centred(key, extent, scale, most, cuts=(), kind=jnp.bfloat16):
    entries = jax.random.normal(key, extent, jnp.float32) * scale
    if len(cuts) > 0:
        entries = level_of(key, extent, cuts, -0.22, 0.18) * entries
    return jnp.clip(entries, min=-most, max=most).astype(kind)


def setup_inputs(seed: int = 0) -> dict:
    arg_keys = jax.random.split(jax.random.key(seed), 9)
    return {
        "queries": draw_queries(jax.random.fold_in(arg_keys[8], 71), 0),
        "keys": draw_keys(jax.random.fold_in(arg_keys[8], 71), 0),
        "values": centred(arg_keys[2], (SEQUENCE_TOKENS, KEY_VALUE_HEADS * HEAD_SIZE), 1.0, 6.0, ((0, 64), (1, 4))),
        "output_gradient": centred(arg_keys[3], (SEQUENCE_TOKENS, QUERY_HEADS * HEAD_SIZE), 1.0, 6.0, ((0, 64), (1, 4))),
        "key_exponents": place_ends(jax.random.randint(arg_keys[4], (SEQUENCE_TOKENS // SCALE_BLOCK, KEY_VALUE_HEADS), -1, 2), jax.random.fold_in(arg_keys[4], 1), -1, 1).astype(jnp.int32),
        "value_exponents": place_ends(jax.random.randint(arg_keys[5], (SEQUENCE_TOKENS // SCALE_BLOCK, KEY_VALUE_HEADS), -1, 2), jax.random.fold_in(arg_keys[5], 1), -1, 1).astype(jnp.int32),
        "key_matrix": centred(arg_keys[6], (MODEL_WIDTH, KEY_VALUE_HEADS * HEAD_SIZE), (KEY_VALUE_HEADS * HEAD_SIZE) ** -0.5, 0.1875, ((1, 4),)),
        "value_matrix": centred(arg_keys[7], (MODEL_WIDTH, KEY_VALUE_HEADS * HEAD_SIZE), (KEY_VALUE_HEADS * HEAD_SIZE) ** -0.5, 0.1875, ((1, 4),)),
    }


def power_of_two(exponents):
    return jnp.where(exponents > 0, 2.0, jnp.where(exponents < 0, 0.5, 1.0)).astype(jnp.float32)


def reference(queries, keys, values, output_gradient, key_exponents, value_exponents, key_matrix, value_matrix):
    score_scale = QUERY_SCALE ** -0.5
    group_width = QUERY_HEADS // KEY_VALUE_HEADS
    key_multiplier = jnp.repeat(power_of_two(key_exponents), SCALE_BLOCK, axis=0)[:, :, None]
    value_multiplier = jnp.repeat(power_of_two(value_exponents), SCALE_BLOCK, axis=0)[:, :, None]
    exact_keys = (keys.astype(jnp.float32).reshape(SEQUENCE_TOKENS, KEY_VALUE_HEADS, HEAD_SIZE) * key_multiplier).astype(jnp.bfloat16)
    exact_values = (values.astype(jnp.float32).reshape(SEQUENCE_TOKENS, KEY_VALUE_HEADS, HEAD_SIZE) * value_multiplier).astype(jnp.bfloat16)
    running_sum = jnp.cumsum(exact_keys.astype(jnp.float32), axis=0)
    preceding = jnp.concatenate([jnp.zeros((ATTEND_WINDOW, KEY_VALUE_HEADS, HEAD_SIZE), jnp.float32), running_sum], 0)[:SEQUENCE_TOKENS]
    places = jnp.arange(SEQUENCE_TOKENS, dtype=jnp.int32)
    counts = jnp.minimum(places + 1, ATTEND_WINDOW).astype(jnp.float32)
    key_mean = (running_sum - preceding) / counts[:, None, None]
    smoothed_keys = (exact_keys.astype(jnp.float32) - key_mean).astype(jnp.bfloat16)

    block_rows = math.gcd(SEQUENCE_TOKENS, 512)
    key_padding = jnp.concatenate([jnp.zeros((ATTEND_WINDOW, KEY_VALUE_HEADS, HEAD_SIZE), jnp.bfloat16), smoothed_keys], 0)
    value_padding = jnp.concatenate([jnp.zeros((ATTEND_WINDOW, KEY_VALUE_HEADS, HEAD_SIZE), jnp.bfloat16), exact_values], 0)
    query_head_count = queries.reshape(SEQUENCE_TOKENS, KEY_VALUE_HEADS, group_width, HEAD_SIZE)
    gradient_heads = output_gradient.reshape(SEQUENCE_TOKENS, KEY_VALUE_HEADS, group_width, HEAD_SIZE)

    def one_block(block_index):
        begin_row = block_index * block_rows
        query_rows = lax.dynamic_slice_in_dim(query_head_count, begin_row, block_rows, 0).astype(jnp.float32)
        grad_rows = lax.dynamic_slice_in_dim(gradient_heads, begin_row, block_rows, 0).astype(jnp.float32)
        key_rows = lax.dynamic_slice_in_dim(key_padding, begin_row, block_rows + ATTEND_WINDOW, 0).astype(jnp.float32)
        value_rows = lax.dynamic_slice_in_dim(value_padding, begin_row, block_rows + ATTEND_WINDOW, 0).astype(jnp.float32)
        query_at = begin_row + jnp.arange(block_rows, dtype=jnp.int32)
        key_at = begin_row - ATTEND_WINDOW + jnp.arange(block_rows + ATTEND_WINDOW, dtype=jnp.int32)
        distance = query_at[:, None] - key_at[None, :]
        allowed = (distance >= 0) & (distance < ATTEND_WINDOW) & (key_at[None, :] >= 0)
        scores = jnp.einsum("qhgd,khd->hgqk", query_rows, key_rows) * score_scale
        scores = jnp.where(allowed, scores, -jnp.inf)
        highest = jnp.max(scores, axis=-1, keepdims=True)
        weights = jnp.exp(scores - highest)
        shares = weights / jnp.sum(weights, axis=-1, keepdims=True)
        rounded = lax.optimization_barrier(shares.astype(jnp.bfloat16)).astype(jnp.float32)
        attended = jnp.einsum("hgqk,khd->hgqd", rounded, value_rows)
        row_dot = jnp.einsum("hgqd,qhgd->hgq", attended, grad_rows)[..., None]
        share_grad = jnp.einsum("qhgd,khd->hgqk", grad_rows, value_rows)
        score_grad = lax.optimization_barrier((shares * (share_grad - row_dot)).astype(jnp.bfloat16)).astype(jnp.float32)
        query_part = (score_scale * jnp.einsum("hgqk,khd->qhgd", score_grad, key_rows)).astype(jnp.bfloat16)
        key_part = score_scale * jnp.einsum("hgqk,qhgd->khd", score_grad, query_rows)
        value_part = jnp.einsum("hgqk,qhgd->khd", rounded, grad_rows)
        return query_part, key_part, value_part

    def advance(carried, block_index):
        key_gradient_sum, value_gradient_sum = carried
        query_part, key_part, value_part = one_block(block_index)
        begin_row = block_index * block_rows
        key_gradient_sum = lax.dynamic_update_slice_in_dim(
            key_gradient_sum, lax.dynamic_slice_in_dim(key_gradient_sum, begin_row, block_rows + ATTEND_WINDOW, 0) + key_part, begin_row, 0)
        value_gradient_sum = lax.dynamic_update_slice_in_dim(
            value_gradient_sum, lax.dynamic_slice_in_dim(value_gradient_sum, begin_row, block_rows + ATTEND_WINDOW, 0) + value_part, begin_row, 0)
        return (key_gradient_sum, value_gradient_sum), query_part

    blank_rows = jnp.zeros((SEQUENCE_TOKENS + ATTEND_WINDOW, KEY_VALUE_HEADS, HEAD_SIZE), jnp.float32)
    (key_gradient_sum, value_gradient_sum), query_parts = lax.scan(
        advance, (blank_rows, blank_rows), jnp.arange(SEQUENCE_TOKENS // block_rows, dtype=jnp.int32))
    query_grad = query_parts.reshape(SEQUENCE_TOKENS, QUERY_HEADS * HEAD_SIZE)
    scaled_keys = (key_gradient_sum[ATTEND_WINDOW:] * key_multiplier).astype(jnp.bfloat16).reshape(SEQUENCE_TOKENS, KEY_VALUE_HEADS * HEAD_SIZE)
    scaled_values = (value_gradient_sum[ATTEND_WINDOW:] * value_multiplier).astype(jnp.bfloat16).reshape(SEQUENCE_TOKENS, KEY_VALUE_HEADS * HEAD_SIZE)

    group_members = KEY_VALUE_HEADS * HEAD_SIZE // N_HEAD
    summed = jnp.zeros((MODEL_WIDTH, SEQUENCE_TOKENS), jnp.float32)
    for group_index in range(N_HEAD):
        first_col = group_index * group_members
        last_col = first_col + group_members
        partial_value = jnp.dot(key_matrix[:, first_col:last_col], scaled_keys[:, first_col:last_col].T,
                          preferred_element_type=jnp.float32)
        partial_value = partial_value + jnp.dot(value_matrix[:, first_col:last_col], scaled_values[:, first_col:last_col].T,
                                    preferred_element_type=jnp.float32)
        summed = summed + lax.optimization_barrier(partial_value.astype(jnp.bfloat16)).astype(jnp.float32)
    return query_grad, summed.astype(jnp.bfloat16)
```

```python
import functools

import jax
import jax.numpy as jnp
from jax import lax
from jax.experimental import pallas as pl
from jax.experimental.pallas import tpu as pltpu
from jax.sharding import PartitionSpec as P

HEAD_SIZE = 128
QUERY_SCALE = 168
ATTEND_WINDOW = 1024
SCALE_BLOCK = 128
TILE = 256
BLOCK = 512
WINDOW_ROWS = 3 * BLOCK
HALF_ROWS = 672
LOG2_E = 1.4426950408889634
MEBI = 1024 * 1024

NN = (((1,), (0,)), ((), ()))
NT = (((1,), (1,)), ((), ()))


def product(left, right, dims):
    return lax.dot_general(left, right, dims, preferred_element_type=jnp.float32)


def vmem_call(kernel, out_shapes, inputs, in_specs=None, scratch=(), mebibytes=8):
    whole = pl.BlockSpec(memory_space=pltpu.VMEM)
    return pl.pallas_call(
        kernel,
        out_shape=out_shapes,
        in_specs=in_specs if in_specs is not None else [whole] * len(inputs),
        out_specs=jax.tree.map(lambda _: whole, out_shapes),
        scratch_shapes=list(scratch),
        cost_estimate=pl.CostEstimate(flops=1, bytes_accessed=1, transcendentals=0),
        compiler_params=pltpu.CompilerParams(vmem_limit_bytes=mebibytes * MEBI),
    )(*inputs)


def shape_of(rows, columns, dtype=jnp.bfloat16):
    return jax.ShapeDtypeStruct((rows, columns), dtype)


SMEM = pl.BlockSpec(memory_space=pltpu.SMEM)
VMEM = pl.BlockSpec(memory_space=pltpu.VMEM)
HBM = pl.BlockSpec(memory_space=pltpu.MemorySpace.HBM)


def factor_of(exponent):
    return jnp.where(exponent > 0, 2.0, jnp.where(exponent < 0, 0.5, 1.0)).astype(jnp.float32)


def dequantize_kernel(key_exps, value_exps, keys, values, key_out, value_out, total_out, key_in, value_in, arrivals):
    fetch_keys = pltpu.make_async_copy(keys, key_in, arrivals.at[0])
    fetch_values = pltpu.make_async_copy(values, value_in, arrivals.at[1])
    fetch_keys.start()
    fetch_values.start()
    for part, (fetch, source, exponents, target) in enumerate(
        ((fetch_keys, key_in, key_exps, key_out), (fetch_values, value_in, value_exps, value_out))
    ):
        fetch.wait()
        for head in range(2):
            lanes = slice(head * HEAD_SIZE, (head + 1) * HEAD_SIZE)
            total = jnp.zeros((1, HEAD_SIZE), jnp.float32)
            for block in range(BLOCK // SCALE_BLOCK):
                rows = slice(block * SCALE_BLOCK, (block + 1) * SCALE_BLOCK)
                scaled = source[rows, lanes].astype(jnp.float32) * factor_of(exponents[head, block])
                target[rows, lanes] = scaled.astype(jnp.bfloat16)
                if part == 0:
                    total = total + jnp.sum(scaled, axis=0, keepdims=True)
            if part == 0:
                total_out[:, lanes] = jnp.broadcast_to(total, (8, HEAD_SIZE))


def smooth_kernel(place, own, older, total, smooth_out):
    first = place[0] * BLOCK
    row = lax.broadcasted_iota(jnp.int32, (BLOCK, BLOCK), 0)
    column = lax.broadcasted_iota(jnp.int32, (BLOCK, BLOCK), 1)
    upto = (column <= row).astype(jnp.float32).astype(jnp.bfloat16)
    after = (column > row).astype(jnp.float32).astype(jnp.bfloat16)
    sums = product(upto, own[...], NN) + product(after, older[...], NN) + total[0:1, :]
    position = first + lax.broadcasted_iota(jnp.int32, (BLOCK, 1), 0)
    counts = jnp.minimum(position + 1, ATTEND_WINDOW).astype(jnp.float32)
    smooth_out[...] = (own[...].astype(jnp.float32) - sums / counts).astype(jnp.bfloat16)


def attend_kernel(
    head, place, queries, grads, keys2, last, keys0, values2, values0,
    query_grad, grad2, grad1, grad0,
    key_rows, value_rows, key_cols, value_cols, weights, shares_out, score_out,
):
    scale = QUERY_SCALE ** (-0.5)
    index = place[0]
    lanes = slice(head * HEAD_SIZE, (head + 1) * HEAD_SIZE)
    last_lanes = slice(256 + head * HEAD_SIZE, 256 + (head + 1) * HEAD_SIZE)
    for at, source in enumerate((keys2, last, keys0)):
        key_rows[at * BLOCK : (at + 1) * BLOCK, :] = source[:, lanes]
    for at, source in enumerate((values2, last, values0)):
        value_rows[at * BLOCK : (at + 1) * BLOCK, :] = source[:, last_lanes if at == 1 else lanes]
    eye = (
        lax.broadcasted_iota(jnp.int32, (HEAD_SIZE, HEAD_SIZE), 0)
        == lax.broadcasted_iota(jnp.int32, (HEAD_SIZE, HEAD_SIZE), 1)
    ).astype(jnp.float32).astype(jnp.bfloat16)
    key_cols[...] = product(eye, key_rows[...], NT).astype(jnp.bfloat16)
    value_cols[...] = product(eye, value_rows[...], NT).astype(jnp.bfloat16)
    key_at = lax.broadcasted_iota(jnp.int32, (TILE, TILE), 0)
    query_at = lax.broadcasted_iota(jnp.int32, (TILE, TILE), 1)
    lowest = -jnp.inf

    for member in range(2):
        for tile in range(BLOCK // TILE):
            rows = slice(tile * TILE, (tile + 1) * TILE)
            columns = slice((2 * head + member) * HEAD_SIZE, (2 * head + member + 1) * HEAD_SIZE)
            query = queries[rows, columns]
            grad = grads[rows, columns]
            grad_cols = product(eye, grad, NT)
            part = 2 * member + tile
            place_at = slice(part * TILE, (part + 1) * TILE)
            valid = [index >= 2, index >= 2, index >= 1, index >= 1, None, None]
            highest = jnp.full((1, TILE), lowest, jnp.float32)
            for step in range(5):
                source = tile + step
                at = slice(step * TILE, (step + 1) * TILE)
                scores = product(key_rows[source * TILE : (source + 1) * TILE, :], query, NT)
                if step == 0:
                    scores = jnp.where(key_at > query_at, scores, lowest)
                if step == 4:
                    scores = jnp.where(key_at <= query_at, scores, lowest)
                weights[part, at, :] = scores
                peak = jnp.max(scores, axis=0, keepdims=True)
                if valid[source] is not None:
                    peak = jnp.where(valid[source], peak, lowest)
                highest = jnp.maximum(highest, peak)
            factor = scale * LOG2_E
            shift = highest * factor
            total = jnp.zeros((1, TILE), jnp.float32)
            for step in range(5):
                source = tile + step
                at = slice(step * TILE, (step + 1) * TILE)
                off = shift if valid[source] is None else jnp.where(valid[source], shift, jnp.inf)
                weight = jnp.exp2(weights[part, at, :] * factor - off)
                weights[part, at, :] = weight
                total = total + jnp.sum(weight, axis=0, keepdims=True)
            inverse = 1.0 / total
            attended = jnp.zeros((HEAD_SIZE, TILE), jnp.float32)
            for step in range(5):
                source = tile + step
                rounded = (weights[part, step * TILE : (step + 1) * TILE, :] * inverse).astype(jnp.bfloat16)
                shares_out[source * TILE : (source + 1) * TILE, place_at] = rounded
                attended = attended + product(value_cols[:, source * TILE : (source + 1) * TILE], rounded, NN)
            row_dot = jnp.sum(attended * grad_cols, axis=0, keepdims=True)
            query_part = jnp.zeros((HEAD_SIZE, TILE), jnp.float32)
            for step in range(5):
                source = tile + step
                share_grad = product(value_rows[source * TILE : (source + 1) * TILE, :], grad, NT)
                share = weights[part, step * TILE : (step + 1) * TILE, :] * inverse
                score_grad = (share * (share_grad - row_dot)).astype(jnp.bfloat16)
                score_out[source * TILE : (source + 1) * TILE, place_at] = score_grad
                query_part = query_part + product(key_cols[:, source * TILE : (source + 1) * TILE], score_grad, NN)
            query_grad[rows, member * HEAD_SIZE : (member + 1) * HEAD_SIZE] = (
                (query_part * scale).T.astype(jnp.bfloat16)
            )

    for source in range(6):
        rows = slice(source * TILE, (source + 1) * TILE)
        out, first = ((grad2, 0), (grad1, 2), (grad0, 4))[source // 2]
        target = slice((source - first) * TILE, (source - first + 1) * TILE)
        if 1 <= source <= 4:
            parts = [(slice(member * BLOCK, (member + 1) * BLOCK), member, slice(0, BLOCK)) for member in range(2)]
        else:
            tile = 0 if source == 0 else 1
            parts = [
                (slice((2 * member + tile) * TILE, (2 * member + tile + 1) * TILE), member, slice(tile * TILE, (tile + 1) * TILE))
                for member in range(2)
            ]
        key_part = jnp.zeros((TILE, HEAD_SIZE), jnp.float32)
        value_part = jnp.zeros((TILE, HEAD_SIZE), jnp.float32)
        for place_at, member, query_rows in parts:
            columns = slice((2 * head + member) * HEAD_SIZE, (2 * head + member + 1) * HEAD_SIZE)
            key_part = key_part + product(score_out[rows, place_at], queries[query_rows, columns], NN)
            value_part = value_part + product(shares_out[rows, place_at], grads[query_rows, columns], NN)
        out[target, 0:HEAD_SIZE] = (key_part * scale).astype(out.dtype)
        out[target, HEAD_SIZE : 2 * HEAD_SIZE] = value_part.astype(out.dtype)


def merge_kernel(place, older, arrived, out):
    odd = (place[0] & 1).astype(jnp.float32)
    out[...] = (older[...] + odd * arrived[...].astype(jnp.float32)).astype(jnp.bfloat16)


def finish_kernel(head, place, key_exps, value_exps, own, sibling, later, out):
    even = (1 - (place[0] & 1)).astype(jnp.float32)
    for block in range(BLOCK // SCALE_BLOCK):
        rows = slice(block * SCALE_BLOCK, (block + 1) * SCALE_BLOCK)
        for part, exponents in ((0, key_exps), (1, value_exps)):
            at = (rows, slice(part * HEAD_SIZE, (part + 1) * HEAD_SIZE))
            total = own[at] + even * sibling[at].astype(jnp.float32) + later[at].astype(jnp.float32)
            out[at] = (total * factor_of(exponents[head, block])).astype(jnp.bfloat16)


def project_kernel(head, place, own, *rest):
    mine, other, pieces, out = rest[:3], rest[3:6], rest[6:10], rest[-1]
    core = place[0] & 1
    half = HALF_ROWS
    lanes = slice(head * HEAD_SIZE, (head + 1) * HEAD_SIZE)
    channels = jnp.concatenate([piece[...] for piece in pieces], axis=1)
    for half_at, matrices in ((core, mine), (1 - core, other)):
        rows = pl.ds(pl.multiple_of(half_at * half, 16), half)
        parts = [own[0, rows, lanes], own[1, rows, lanes]]
        for matrix in matrices:
            parts += [matrix[0:half, lanes], matrix[half : 2 * half, lanes]]
        total = product(jnp.concatenate(parts, axis=1), channels, NT)
        if len(rest) == 12:
            total = total + rest[10][rows, :]
        out[rows, :] = total.astype(out.dtype)


def fetch_kernel(place, keys, values, queries, grads, ready, sent1, sent2, sent3, own, query_out, grad_out, arrivals):
    half = HALF_ROWS
    core = place[0] & 1
    copies = []
    for steps, target in ((1, sent1), (2, sent2), (3, sent3)):
        begin = pl.multiple_of(((place[1] + steps) & 3) * (2 * half) + core * half, 16)
        for part, matrix in enumerate((keys, values)):
            copies.append((matrix.at[pl.ds(begin, half), :], target.at[pl.ds(part * half, half), :]))
    begin = pl.multiple_of(place[1] * (2 * half), 16)
    for part, matrix in enumerate((keys, values)):
        copies.append((matrix.at[pl.ds(begin, 2 * half), :], own.at[part]))
    copies += [(queries, query_out), (grads, grad_out)]
    started = [pltpu.make_async_copy(*pair, arrivals.at[at]) for at, pair in enumerate(copies)]
    for copy in started:
        copy.start()
    for copy in started:
        copy.wait()


def shift_pairs(count, steps):
    return [(at, at + steps) for at in range(max(0, -steps), min(count, count - steps))]


def local(
    queries, keys, values, output_gradient, key_exponents, value_exponents, key_matrix, value_matrix
):
    count = lax.axis_size("seq")
    groups = lax.axis_size("head")
    index = lax.axis_index("seq")
    place = jnp.stack([index, lax.axis_index("head")]).astype(jnp.int32)
    core = index & 1
    siblings = [(at, at ^ 1) for at in range(count)]

    def to_sibling(value):
        return lax.ppermute(value, "seq", siblings)

    def onward(value, steps):
        return lax.ppermute(value, "seq", shift_pairs(count, steps))

    key_exponents, value_exponents = key_exponents.T, value_exponents.T
    exact_keys, exact_values, key_total = vmem_call(
        dequantize_kernel,
        (shape_of(BLOCK, 256), shape_of(BLOCK, 256), shape_of(8, 256, jnp.float32)),
        (key_exponents, value_exponents, keys, values),
        in_specs=[SMEM, SMEM, HBM, HBM],
        mebibytes=60,
        scratch=[
            pltpu.VMEM((BLOCK, 256), jnp.bfloat16),
            pltpu.VMEM((BLOCK, 256), jnp.bfloat16),
            pltpu.SemaphoreType.DMA((2,)),
        ],
    )
    older_keys = onward(exact_keys, 2)
    last_total = onward(key_total, 1)

    model_rows = key_matrix.shape[0] // groups
    piece_shape = shape_of(model_rows, 256)
    *sent, own, queries, output_gradient = vmem_call(
        fetch_kernel,
        (piece_shape, piece_shape, piece_shape, jax.ShapeDtypeStruct((2, model_rows, 256), jnp.bfloat16), shape_of(BLOCK, 512), shape_of(BLOCK, 512)),
        (place, key_matrix, value_matrix, queries, output_gradient, exact_keys),
        in_specs=[SMEM] + [HBM] * 4 + [pl.BlockSpec(memory_space=pl.ANY)],
        scratch=[pltpu.SemaphoreType.DMA((10,))],
        mebibytes=57,
    )
    fetched = [
        lax.ppermute(piece, "head", [(at, (at + steps) % groups) for at in range(groups)])
        for steps, piece in zip(range(1, groups), sent)
    ]

    late_values, _ = lax.optimization_barrier((exact_values, last_total))
    older_values = onward(late_values, 2)
    older_keys, _ = lax.optimization_barrier((older_keys, own))
    smooth = vmem_call(
        smooth_kernel, shape_of(BLOCK, 256), (place, exact_keys, older_keys, last_total), in_specs=[SMEM, VMEM, VMEM, VMEM]
    )
    older_smooth = onward(smooth, 2)
    last = to_sibling(
        jnp.where(
            core == 0,
            jnp.concatenate([smooth, exact_values], axis=1),
            jnp.concatenate([older_smooth, older_values], axis=1),
        )
    )

    query_grads, gathered = [], []
    for head in range(2):
        if head == 1:
            queries, _ = lax.optimization_barrier((queries, back))
        query_part, grad2, grad1, grad0 = vmem_call(
            functools.partial(attend_kernel, head),
            (shape_of(BLOCK, 256), shape_of(BLOCK, 256, jnp.float32), shape_of(BLOCK, 256), shape_of(BLOCK, 256, jnp.float32)),
            (place, queries, output_gradient, older_smooth, last, smooth, older_values, exact_values),
            in_specs=[SMEM] + [VMEM] * 7,
            scratch=[
                pltpu.VMEM((WINDOW_ROWS, HEAD_SIZE), jnp.bfloat16),
                pltpu.VMEM((WINDOW_ROWS, HEAD_SIZE), jnp.bfloat16),
                pltpu.VMEM((HEAD_SIZE, WINDOW_ROWS), jnp.bfloat16),
                pltpu.VMEM((HEAD_SIZE, WINDOW_ROWS), jnp.bfloat16),
                pltpu.VMEM((4, 5 * TILE, TILE), jnp.float32),
                pltpu.VMEM((WINDOW_ROWS, 4 * TILE), jnp.bfloat16),
                pltpu.VMEM((WINDOW_ROWS, 4 * TILE), jnp.bfloat16),
            ],
            mebibytes=18,
        )
        query_grads.append(query_part)
        sibling_grad = to_sibling(grad1)
        back = vmem_call(merge_kernel, shape_of(BLOCK, 256), (place, grad2, sibling_grad), in_specs=[SMEM, VMEM, VMEM])
        later_grad = onward(back, -2)
        scaled = vmem_call(
            functools.partial(finish_kernel, head),
            shape_of(BLOCK, 256),
            (place, key_exponents, value_exponents, grad0, sibling_grad, later_grad),
            in_specs=[SMEM, SMEM, SMEM, VMEM, VMEM, VMEM],
        )
        arrived = [scaled]
        for steps in (1, 2, 3):
            pairs = [(at, (at + steps) % groups) for at in range(groups)]
            arrived.append(lax.ppermute(scaled, "head", pairs))
        gathered.append(arrived)
    fetched = lax.optimization_barrier((*fetched, gathered[0][0]))[:-1]
    swapped = [to_sibling(piece) for piece in fetched]
    input_grad = None
    for head in range(2):
        more = () if input_grad is None else (input_grad,)
        input_grad = vmem_call(
            functools.partial(project_kernel, head),
            shape_of(model_rows, BLOCK, jnp.bfloat16 if head else jnp.float32),
            (place, own, *fetched, *swapped, *gathered[head], *more),
            in_specs=[SMEM] + [VMEM] * (11 + len(more)),
            mebibytes=18,
        )
    return jnp.concatenate(query_grads, axis=1), input_grad


def solution(mesh):
    in_specs = (
        P("seq", "head"),
        P("seq", "head"),
        P("seq", "head"),
        P("seq", "head"),
        P("seq", "head"),
        P("seq", "head"),
        P(None, "head"),
        P(None, "head"),
    )
    out_specs = (P("seq", "head"), P("head", "seq"))
    return jax.shard_map(local, mesh=mesh, in_specs=in_specs, out_specs=out_specs, check_vma=False)
```

```python
import functools

import jax
import jax.numpy as jnp
from jax import lax
from jax.experimental import pallas as pl
from jax.experimental.pallas import tpu as pltpu
from jax.sharding import PartitionSpec as P

HEAD_SIZE = 128
QUERY_SCALE = 168
ATTEND_WINDOW = 1024
SCALE_BLOCK = 128
TILE = 256
BLOCK = 512
WINDOW_ROWS = 3 * BLOCK
HALF_ROWS = 672
LOG2_E = 1.4426950408889634
MEBI = 1024 * 1024

NN = (((1,), (0,)), ((), ()))
NT = (((1,), (1,)), ((), ()))


def product(left, right, dims):
    return lax.dot_general(left, right, dims, preferred_element_type=jnp.float32)


def vmem_call(kernel, out_shapes, inputs, in_specs=None, scratch=(), mebibytes=8, flops=1):
    whole = pl.BlockSpec(memory_space=pltpu.VMEM)
    return pl.pallas_call(
        kernel,
        out_shape=out_shapes,
        in_specs=in_specs if in_specs is not None else [whole] * len(inputs),
        out_specs=jax.tree.map(lambda _: whole, out_shapes),
        scratch_shapes=list(scratch),
        cost_estimate=pl.CostEstimate(flops=flops, bytes_accessed=1, transcendentals=0),
        compiler_params=pltpu.CompilerParams(vmem_limit_bytes=mebibytes * MEBI),
    )(*inputs)


def shape_of(rows, columns, dtype=jnp.bfloat16):
    return jax.ShapeDtypeStruct((rows, columns), dtype)


SMEM = pl.BlockSpec(memory_space=pltpu.SMEM)
VMEM = pl.BlockSpec(memory_space=pltpu.VMEM)
HBM = pl.BlockSpec(memory_space=pltpu.MemorySpace.HBM)


def factor_of(exponent):
    return jnp.where(exponent > 0, 2.0, jnp.where(exponent < 0, 0.5, 1.0)).astype(jnp.float32)


def identity():
    row = lax.broadcasted_iota(jnp.int32, (HEAD_SIZE, HEAD_SIZE), 0)
    column = lax.broadcasted_iota(jnp.int32, (HEAD_SIZE, HEAD_SIZE), 1)
    return (row == column).astype(jnp.float32).astype(jnp.bfloat16)


def front_kernel(
    index, group, key_exps, value_exps, keys, values, key_matrix, value_matrix,
    key_out, value_out, total_out, sent1, sent2, sent3,
    key_in, value_in, rows, arrivals, departures,
):
    fetch_keys = pltpu.make_async_copy(keys, key_in, arrivals.at[0])
    fetch_values = pltpu.make_async_copy(values, value_in, arrivals.at[1])
    fetch_keys.start()
    fetch_values.start()
    half = HALF_ROWS
    core = index[0] & 1
    incoming, outgoing = [], []
    for at, (steps, target) in enumerate(((1, sent1), (3, sent3), (2, sent2))):
        begin = pl.multiple_of(((group[0] + steps) & 3) * (2 * half) + core * half, 16)
        for part, matrix in enumerate((key_matrix, value_matrix)):
            incoming.append(
                pltpu.make_async_copy(
                    matrix.at[pl.ds(begin, half), :], rows.at[at, pl.ds(part * half, half), :], arrivals.at[2 + 2 * at + part]
                )
            )
        outgoing.append(pltpu.make_async_copy(rows.at[at], target, departures.at[at]))
    for copy in incoming:
        copy.start()
    for part, (fetch, source, exponents, target) in enumerate(
        ((fetch_keys, key_in, key_exps, key_out), (fetch_values, value_in, value_exps, value_out))
    ):
        fetch.wait()
        for head in range(2):
            lanes = slice(head * HEAD_SIZE, (head + 1) * HEAD_SIZE)
            total = jnp.zeros((1, HEAD_SIZE), jnp.float32)
            for block in range(BLOCK // SCALE_BLOCK):
                rows_at = slice(block * SCALE_BLOCK, (block + 1) * SCALE_BLOCK)
                scaled = source[rows_at, lanes].astype(jnp.float32) * factor_of(exponents[head, block])
                target[rows_at, lanes] = scaled.astype(jnp.bfloat16)
                if part == 0:
                    total = total + jnp.sum(scaled, axis=0, keepdims=True)
            if part == 0:
                total_out[:, lanes] = jnp.broadcast_to(total, (8, HEAD_SIZE))
    for at in range(3):
        incoming[2 * at].wait()
        incoming[2 * at + 1].wait()
        outgoing[at].start()
    for copy in outgoing:
        copy.wait()


def smooth_kernel(place, own, older, total, smooth_out):
    first = place[0] * BLOCK
    row = lax.broadcasted_iota(jnp.int32, (BLOCK, BLOCK), 0)
    column = lax.broadcasted_iota(jnp.int32, (BLOCK, BLOCK), 1)
    upto = (column <= row).astype(jnp.float32).astype(jnp.bfloat16)
    after = (column > row).astype(jnp.float32).astype(jnp.bfloat16)
    sums = product(upto, own[...], NN) + product(after, older[...], NN) + total[0:1, :]
    position = first + lax.broadcasted_iota(jnp.int32, (BLOCK, 1), 0)
    counts = jnp.minimum(position + 1, ATTEND_WINDOW).astype(jnp.float32)
    smooth_out[...] = (own[...].astype(jnp.float32) - sums / counts).astype(jnp.bfloat16)


def attend_kernel(
    head, place, queries, grads, all_grad_cols, keys2, last, keys0, values2, values0,
    query_grad, grad2, grad1, grad0,
    key_rows, value_rows, key_cols, value_cols, weights, shares_out, score_out,
):
    scale = QUERY_SCALE ** (-0.5)
    index = place[0]
    lanes = slice(head * HEAD_SIZE, (head + 1) * HEAD_SIZE)
    last_lanes = slice(256 + head * HEAD_SIZE, 256 + (head + 1) * HEAD_SIZE)
    for at, source in enumerate((keys2, last, keys0)):
        key_rows[at * BLOCK : (at + 1) * BLOCK, :] = source[:, lanes]
    for at, source in enumerate((values2, last, values0)):
        value_rows[at * BLOCK : (at + 1) * BLOCK, :] = source[:, last_lanes if at == 1 else lanes]
    eye = identity()
    key_cols[...] = product(eye, key_rows[...], NT).astype(jnp.bfloat16)
    value_cols[...] = product(eye, value_rows[...], NT).astype(jnp.bfloat16)
    key_at = lax.broadcasted_iota(jnp.int32, (TILE, TILE), 0)
    query_at = lax.broadcasted_iota(jnp.int32, (TILE, TILE), 1)
    lowest = -jnp.inf

    for member in range(2):
        for tile in range(BLOCK // TILE):
            rows = slice(tile * TILE, (tile + 1) * TILE)
            columns = slice((2 * head + member) * HEAD_SIZE, (2 * head + member + 1) * HEAD_SIZE)
            query = queries[rows, columns]
            grad = grads[rows, columns]
            grad_cols = all_grad_cols[columns, rows]
            part = 2 * member + tile
            place_at = slice(part * TILE, (part + 1) * TILE)
            valid = [index >= 2, index >= 2, index >= 1, index >= 1, None, None]
            highest = jnp.full((1, TILE), lowest, jnp.float32)
            for step in range(5):
                source = tile + step
                at = slice(step * TILE, (step + 1) * TILE)
                scores = product(key_rows[source * TILE : (source + 1) * TILE, :], query, NT)
                if step == 0:
                    scores = jnp.where(key_at > query_at, scores, lowest)
                if step == 4:
                    scores = jnp.where(key_at <= query_at, scores, lowest)
                weights[part, at, :] = scores
                peak = jnp.max(scores, axis=0, keepdims=True)
                if valid[source] is not None:
                    peak = jnp.where(valid[source], peak, lowest)
                highest = jnp.maximum(highest, peak)
            factor = scale * LOG2_E
            shift = highest * factor
            total = jnp.zeros((1, TILE), jnp.float32)
            for step in range(5):
                source = tile + step
                at = slice(step * TILE, (step + 1) * TILE)
                off = shift if valid[source] is None else jnp.where(valid[source], shift, jnp.inf)
                weight = jnp.exp2(weights[part, at, :] * factor - off)
                weights[part, at, :] = weight
                total = total + jnp.sum(weight, axis=0, keepdims=True)
            inverse = 1.0 / total
            attended = jnp.zeros((HEAD_SIZE, TILE), jnp.float32)
            for step in range(5):
                source = tile + step
                rounded = (weights[part, step * TILE : (step + 1) * TILE, :] * inverse).astype(jnp.bfloat16)
                shares_out[source * TILE : (source + 1) * TILE, place_at] = rounded
                attended = attended + product(value_cols[:, source * TILE : (source + 1) * TILE], rounded, NN)
            row_dot = jnp.sum(attended * grad_cols, axis=0, keepdims=True)
            query_part = jnp.zeros((HEAD_SIZE, TILE), jnp.float32)
            for step in range(5):
                source = tile + step
                share_grad = product(value_rows[source * TILE : (source + 1) * TILE, :], grad, NT)
                share = weights[part, step * TILE : (step + 1) * TILE, :] * inverse
                score_grad = (share * (share_grad - row_dot)).astype(jnp.bfloat16)
                score_out[source * TILE : (source + 1) * TILE, place_at] = score_grad
                query_part = query_part + product(key_cols[:, source * TILE : (source + 1) * TILE], score_grad, NN)
            query_grad[rows, member * HEAD_SIZE : (member + 1) * HEAD_SIZE] = (
                (query_part * scale).T.astype(jnp.bfloat16)
            )

    for source in range(6):
        rows = slice(source * TILE, (source + 1) * TILE)
        out, first = ((grad2, 0), (grad1, 2), (grad0, 4))[source // 2]
        target = slice((source - first) * TILE, (source - first + 1) * TILE)
        if 1 <= source <= 4:
            parts = [(slice(member * BLOCK, (member + 1) * BLOCK), member, slice(0, BLOCK)) for member in range(2)]
        else:
            tile = 0 if source == 0 else 1
            parts = [
                (slice((2 * member + tile) * TILE, (2 * member + tile + 1) * TILE), member, slice(tile * TILE, (tile + 1) * TILE))
                for member in range(2)
            ]
        key_part = jnp.zeros((TILE, HEAD_SIZE), jnp.float32)
        value_part = jnp.zeros((TILE, HEAD_SIZE), jnp.float32)
        for place_at, member, query_rows in parts:
            columns = slice((2 * head + member) * HEAD_SIZE, (2 * head + member + 1) * HEAD_SIZE)
            key_part = key_part + product(score_out[rows, place_at], queries[query_rows, columns], NN)
            value_part = value_part + product(shares_out[rows, place_at], grads[query_rows, columns], NN)
        out[target, 0:HEAD_SIZE] = (key_part * scale).astype(out.dtype)
        out[target, HEAD_SIZE : 2 * HEAD_SIZE] = value_part.astype(out.dtype)


def merge_kernel(place, older, arrived, out):
    odd = (place[0] & 1).astype(jnp.float32)
    out[...] = (older[...] + odd * arrived[...].astype(jnp.float32)).astype(jnp.bfloat16)


def finish_kernel(head, place, key_exps, value_exps, own, sibling, later, out):
    even = (1 - (place[0] & 1)).astype(jnp.float32)
    for block in range(BLOCK // SCALE_BLOCK):
        rows = slice(block * SCALE_BLOCK, (block + 1) * SCALE_BLOCK)
        for part, exponents in ((0, key_exps), (1, value_exps)):
            at = (rows, slice(part * HEAD_SIZE, (part + 1) * HEAD_SIZE))
            total = own[at] + even * sibling[at].astype(jnp.float32) + later[at].astype(jnp.float32)
            out[at] = (total * factor_of(exponents[head, block])).astype(jnp.bfloat16)


def remote_part(place, head, half_at, pieces, mine, other):
    half = HALF_ROWS
    lanes = slice(head * HEAD_SIZE, (head + 1) * HEAD_SIZE)
    parts = []
    for matrix in mine if half_at == 0 else other:
        parts += [matrix[0:half, lanes], matrix[half : 2 * half, lanes]]
    return product(jnp.concatenate(parts, axis=1), jnp.concatenate([piece[...] for piece in pieces], axis=1), NT)


def half_slice(place, half_at):
    core = place[0] & 1
    at = core if half_at == 0 else 1 - core
    return pl.ds(pl.multiple_of(at * HALF_ROWS, 16), HALF_ROWS)


def early_kernel(place, group, keys, values, own0, own1, *rest):
    pieces, mine, other, out, rows, arrivals = rest[:3], rest[3:6], rest[6:9], rest[9], rest[10], rest[11]
    begin = pl.multiple_of(group[0] * (2 * HALF_ROWS), 16)
    copies = [
        pltpu.make_async_copy(matrix.at[pl.ds(begin, 2 * HALF_ROWS), :], rows.at[part], arrivals.at[part])
        for part, matrix in enumerate((keys, values))
    ]
    for copy in copies:
        copy.start()
    for half_at in range(2):
        out[half_slice(place, half_at), :] = remote_part(place, 0, half_at, pieces, mine, other)
    for copy in copies:
        copy.wait()
    channels = jnp.concatenate(
        [own0[:, :HEAD_SIZE], own1[:, :HEAD_SIZE], own0[:, HEAD_SIZE:], own1[:, HEAD_SIZE:]], axis=1
    )
    for half_at in range(2):
        at = slice(half_at * HALF_ROWS, (half_at + 1) * HALF_ROWS)
        out[at, :] += product(jnp.concatenate([rows[0, at, :], rows[1, at, :]], axis=1), channels, NT)


def late_kernel(place, early, *rest):
    pieces, mine, other, out = rest[:3], rest[3:6], rest[6:9], rest[9]
    for half_at in range(2):
        rows = half_slice(place, half_at)
        out[rows, :] = (early[rows, :] + remote_part(place, 1, half_at, pieces, mine, other)).astype(out.dtype)


def prepare_kernel(queries, grads, ready, query_out, grad_out, grad_cols):
    query_out[...] = queries[...]
    grad_out[...] = grads[...]
    eye = identity()
    for head in range(4):
        lanes = slice(head * HEAD_SIZE, (head + 1) * HEAD_SIZE)
        grad_cols[lanes, :] = product(eye, grads[:, lanes], NT)


def shift_pairs(count, steps):
    return [(at, at + steps) for at in range(max(0, -steps), min(count, count - steps))]


def local(
    queries, keys, values, output_gradient, key_exponents, value_exponents, key_matrix, value_matrix
):
    count = lax.axis_size("seq")
    groups = lax.axis_size("head")
    index = lax.axis_index("seq")
    place = index.astype(jnp.int32).reshape(1)
    group = lax.axis_index("head").astype(jnp.int32).reshape(1)
    core = index & 1
    siblings = [(at, at ^ 1) for at in range(count)]

    def to_sibling(value):
        return lax.ppermute(value, "seq", siblings)

    def onward(value, steps):
        return lax.ppermute(value, "seq", shift_pairs(count, steps))

    key_exponents, value_exponents = key_exponents.T, value_exponents.T
    model_rows = key_matrix.shape[0] // groups
    piece_shape = shape_of(model_rows, 256)
    exact_keys, exact_values, key_total, *sent = pl.pallas_call(
        front_kernel,
        out_shape=(shape_of(BLOCK, 256), shape_of(BLOCK, 256), shape_of(8, 256, jnp.float32)) + (piece_shape,) * 3,
        in_specs=[SMEM] * 4 + [HBM] * 4,
        out_specs=(VMEM,) * 3 + (HBM,) * 3,
        scratch_shapes=[
            pltpu.VMEM((BLOCK, 256), jnp.bfloat16),
            pltpu.VMEM((BLOCK, 256), jnp.bfloat16),
            pltpu.VMEM((3, model_rows, 256), jnp.bfloat16),
            pltpu.SemaphoreType.DMA((8,)),
            pltpu.SemaphoreType.DMA((3,)),
        ],
        cost_estimate=pl.CostEstimate(flops=1, bytes_accessed=1, transcendentals=0),
        compiler_params=pltpu.CompilerParams(vmem_limit_bytes=59 * MEBI),
    )(place, group, key_exponents, value_exponents, keys, values, key_matrix, value_matrix)
    older_keys = onward(exact_keys, 2)
    last_total = onward(key_total, 1)

    def along_head(value, steps):
        return lax.ppermute(value, "head", [(at, (at + steps) % groups) for at in range(groups)])


    older_values = onward(exact_values, 2)
    smooth = vmem_call(
        smooth_kernel, shape_of(BLOCK, 256), (place, exact_keys, older_keys, last_total), in_specs=[SMEM, VMEM, VMEM, VMEM]
    )
    older_smooth = onward(smooth, 2)
    near, back_near, _ = lax.optimization_barrier((sent[0], sent[2], smooth))
    fetched = [along_head(near, 1), None, along_head(back_near, 3)]
    last = to_sibling(
        jnp.where(
            core == 0,
            jnp.concatenate([smooth, exact_values], axis=1),
            jnp.concatenate([older_smooth, older_values], axis=1),
        )
    )

    queries, output_gradient, grad_cols = vmem_call(
        prepare_kernel,
        (shape_of(BLOCK, 512), shape_of(BLOCK, 512), shape_of(512, BLOCK, jnp.float32)),
        (queries, output_gradient, smooth),
        in_specs=[VMEM, VMEM, pl.BlockSpec(memory_space=pl.ANY)],
    )

    query_grads, gathered = [], []
    for head in range(2):
        if head == 1:
            queries, _, swapped[0], swapped[2] = lax.optimization_barrier((queries, back, swapped[0], swapped[2]))
        query_part, grad2, grad1, grad0 = vmem_call(
            functools.partial(attend_kernel, head),
            (shape_of(BLOCK, 256), shape_of(BLOCK, 256, jnp.float32), shape_of(BLOCK, 256), shape_of(BLOCK, 256, jnp.float32)),
            (place, queries, output_gradient, grad_cols, older_smooth, last, smooth, older_values, exact_values),
            in_specs=[SMEM] + [VMEM] * 8,
            scratch=[
                pltpu.VMEM((WINDOW_ROWS, HEAD_SIZE), jnp.bfloat16),
                pltpu.VMEM((WINDOW_ROWS, HEAD_SIZE), jnp.bfloat16),
                pltpu.VMEM((HEAD_SIZE, WINDOW_ROWS), jnp.bfloat16),
                pltpu.VMEM((HEAD_SIZE, WINDOW_ROWS), jnp.bfloat16),
                pltpu.VMEM((4, 5 * TILE, TILE), jnp.float32),
                pltpu.VMEM((WINDOW_ROWS, 4 * TILE), jnp.bfloat16),
                pltpu.VMEM((WINDOW_ROWS, 4 * TILE), jnp.bfloat16),
            ],
            mebibytes=18,
        )
        query_grads.append(query_part)
        if head == 0:
            fetched[0], fetched[1], fetched[2], _ = lax.optimization_barrier((fetched[0], sent[1], fetched[2], grad1))
            fetched[1] = along_head(fetched[1], 2)
            swapped = [to_sibling(fetched[0]), None, to_sibling(fetched[2])]
        sibling_grad = to_sibling(grad1)
        if head == 1:
            grad2, _ = lax.optimization_barrier((grad2, gathered[0][0]))
        back = vmem_call(merge_kernel, shape_of(BLOCK, 256), (place, grad2, sibling_grad), in_specs=[SMEM, VMEM, VMEM])
        later_grad = onward(back, -2)
        scaled = vmem_call(
            functools.partial(finish_kernel, head),
            shape_of(BLOCK, 256),
            (place, key_exponents, value_exponents, grad0, sibling_grad, later_grad),
            in_specs=[SMEM, SMEM, SMEM, VMEM, VMEM, VMEM],
        )
        arrived = [scaled]
        for steps in (1, 2, 3):
            arrived.append(along_head(scaled, steps))
        gathered.append(arrived)
    fetched[1], _ = lax.optimization_barrier((fetched[1], back))
    swapped[1] = to_sibling(fetched[1])
    early = vmem_call(
        early_kernel,
        shape_of(model_rows, BLOCK, jnp.float32),
        (place, group, key_matrix, value_matrix, gathered[0][0], gathered[1][0], *gathered[0][1:], *fetched, *swapped),
        in_specs=[SMEM, SMEM, HBM, HBM] + [VMEM] * 11,
        scratch=[pltpu.VMEM((2, model_rows, 256), jnp.bfloat16), pltpu.SemaphoreType.DMA((2,))],
        mebibytes=18,
    )
    input_grad = vmem_call(
        late_kernel,
        shape_of(model_rows, BLOCK),
        (place, early, *gathered[1][1:], *fetched, *swapped),
        in_specs=[SMEM] + [VMEM] * 10,
        mebibytes=18,
    )
    return jnp.concatenate(query_grads, axis=1), input_grad


def solution(mesh):
    in_specs = (
        P("seq", "head"),
        P("seq", "head"),
        P("seq", "head"),
        P("seq", "head"),
        P("seq", "head"),
        P("seq", "head"),
        P(None, "head"),
        P(None, "head"),
    )
    out_specs = (P("seq", "head"), P("head", "seq"))
    return jax.shard_map(local, mesh=mesh, in_specs=in_specs, out_specs=out_specs, check_vma=False)
```

```python
import functools

import jax
import jax.numpy as jnp
from jax import lax
from jax.experimental import pallas as pl
from jax.experimental.pallas import tpu as pltpu
from jax.sharding import PartitionSpec as P

HEAD_SIZE = 128
QUERY_SCALE = 168
ATTEND_WINDOW = 1024
SCALE_BLOCK = 128
TILE = 256
BLOCK = 512
WINDOW_ROWS = 3 * BLOCK
HALF_ROWS = 672
LOG2_E = 1.4426950408889634
MEBI = 1024 * 1024
CUT_LIMIT = 57

NN = (((1,), (0,)), ((), ()))
NT = (((1,), (1,)), ((), ()))


def product(left, right, dims):
    return lax.dot_general(left, right, dims, preferred_element_type=jnp.float32)


def vmem_call(kernel, out_shapes, inputs, in_specs=None, scratch=(), mebibytes=8, flops=1):
    whole = pl.BlockSpec(memory_space=pltpu.VMEM)
    return pl.pallas_call(
        kernel,
        out_shape=out_shapes,
        in_specs=in_specs if in_specs is not None else [whole] * len(inputs),
        out_specs=jax.tree.map(lambda _: whole, out_shapes),
        scratch_shapes=list(scratch),
        cost_estimate=pl.CostEstimate(flops=flops, bytes_accessed=1, transcendentals=0),
        compiler_params=pltpu.CompilerParams(vmem_limit_bytes=mebibytes * MEBI),
    )(*inputs)


def shape_of(rows, columns, dtype=jnp.bfloat16):
    return jax.ShapeDtypeStruct((rows, columns), dtype)


SMEM = pl.BlockSpec(memory_space=pltpu.SMEM)
VMEM = pl.BlockSpec(memory_space=pltpu.VMEM)
HBM = pl.BlockSpec(memory_space=pltpu.MemorySpace.HBM)


def factor_of(exponent):
    return jnp.where(exponent > 0, 2.0, jnp.where(exponent < 0, 0.5, 1.0)).astype(jnp.float32)


def identity():
    row = lax.broadcasted_iota(jnp.int32, (HEAD_SIZE, HEAD_SIZE), 0)
    column = lax.broadcasted_iota(jnp.int32, (HEAD_SIZE, HEAD_SIZE), 1)
    return (row == column).astype(jnp.float32).astype(jnp.bfloat16)


def dequantize_kernel(key_exps, value_exps, keys, values, key_out, value_out, total_out):
    for part, (source, exponents, target) in enumerate(((keys, key_exps, key_out), (values, value_exps, value_out))):
        for head in range(2):
            lanes = slice(head * HEAD_SIZE, (head + 1) * HEAD_SIZE)
            total = jnp.zeros((1, HEAD_SIZE), jnp.float32)
            for block in range(BLOCK // SCALE_BLOCK):
                rows = slice(block * SCALE_BLOCK, (block + 1) * SCALE_BLOCK)
                scaled = source[rows, lanes].astype(jnp.float32) * factor_of(exponents[head, block])
                target[rows, lanes] = scaled.astype(jnp.bfloat16)
                if part == 0:
                    total = total + jnp.sum(scaled, axis=0, keepdims=True)
            if part == 0:
                total_out[:, lanes] = jnp.broadcast_to(total, (8, HEAD_SIZE))


def cut_kernel(index, group, key_matrix, value_matrix, ready, sent1, sent2, sent3, rows, arrivals, departures):
    half = HALF_ROWS
    core = index[0] & 1
    incoming, outgoing = [], []
    for at, (steps, target) in enumerate(((1, sent1), (3, sent3), (2, sent2))):
        begin = pl.multiple_of(((group[0] + steps) & 3) * (2 * half) + core * half, 16)
        for part, matrix in enumerate((key_matrix, value_matrix)):
            incoming.append(
                pltpu.make_async_copy(
                    matrix.at[pl.ds(begin, half), :], rows.at[at, pl.ds(part * half, half), :], arrivals.at[2 * at + part]
                )
            )
        outgoing.append(pltpu.make_async_copy(rows.at[at], target, departures.at[at]))
    for copy in incoming:
        copy.start()
    for at in range(3):
        incoming[2 * at].wait()
        incoming[2 * at + 1].wait()
        outgoing[at].start()
    for copy in outgoing:
        copy.wait()


def smooth_kernel(place, own, older, total, smooth_out):
    first = place[0] * BLOCK
    row = lax.broadcasted_iota(jnp.int32, (BLOCK, BLOCK), 0)
    column = lax.broadcasted_iota(jnp.int32, (BLOCK, BLOCK), 1)
    upto = (column <= row).astype(jnp.float32).astype(jnp.bfloat16)
    after = (column > row).astype(jnp.float32).astype(jnp.bfloat16)
    sums = product(upto, own[...], NN) + product(after, older[...], NN) + total[0:1, :]
    position = first + lax.broadcasted_iota(jnp.int32, (BLOCK, 1), 0)
    counts = jnp.minimum(position + 1, ATTEND_WINDOW).astype(jnp.float32)
    smooth_out[...] = (own[...].astype(jnp.float32) - sums / counts).astype(jnp.bfloat16)


def attend_kernel(
    head, place, queries, grads, all_grad_cols, keys2, last, keys0, values2, values0,
    query_grad, grad2, grad1, grad0,
    key_rows, value_rows, key_cols, value_cols, weights, shares_out, score_out,
):
    scale = QUERY_SCALE ** (-0.5)
    index = place[0]
    lanes = slice(head * HEAD_SIZE, (head + 1) * HEAD_SIZE)
    last_lanes = slice(256 + head * HEAD_SIZE, 256 + (head + 1) * HEAD_SIZE)
    for at, source in enumerate((keys2, last, keys0)):
        key_rows[at * BLOCK : (at + 1) * BLOCK, :] = source[:, lanes]
    for at, source in enumerate((values2, last, values0)):
        value_rows[at * BLOCK : (at + 1) * BLOCK, :] = source[:, last_lanes if at == 1 else lanes]
    eye = identity()
    key_cols[...] = product(eye, key_rows[...], NT).astype(jnp.bfloat16)
    value_cols[...] = product(eye, value_rows[...], NT).astype(jnp.bfloat16)
    key_at = lax.broadcasted_iota(jnp.int32, (TILE, TILE), 0)
    query_at = lax.broadcasted_iota(jnp.int32, (TILE, TILE), 1)
    lowest = -jnp.inf

    valid = [index >= 2, index >= 2, index >= 1, index >= 1, None, None]
    factor = scale * LOG2_E
    parts = []
    for tile in range(BLOCK // TILE):
        for member in range(2):
            part = 2 * member + tile
            rows = slice(tile * TILE, (tile + 1) * TILE)
            columns = slice((2 * head + member) * HEAD_SIZE, (2 * head + member + 1) * HEAD_SIZE)
            parts.append(dict(
                part=part, tile=tile, member=member, rows=rows, columns=columns,
                highest=jnp.full((1, TILE), lowest, jnp.float32),
                total=jnp.zeros((1, TILE), jnp.float32),
                attended=jnp.zeros((HEAD_SIZE, TILE), jnp.float32),
                query_part=jnp.zeros((HEAD_SIZE, TILE), jnp.float32),
            ))

    def take_scores(now, step):
        source, part = now["tile"] + step, now["part"]
        scores = product(key_rows[source * TILE : (source + 1) * TILE, :], queries[now["rows"], now["columns"]], NT)
        if step == 0:
            scores = jnp.where(key_at > query_at, scores, lowest)
        if step == 4:
            scores = jnp.where(key_at <= query_at, scores, lowest)
        weights[part, step * TILE : (step + 1) * TILE, :] = scores
        peak = jnp.max(scores, axis=0, keepdims=True)
        if valid[source] is not None:
            peak = jnp.where(valid[source], peak, lowest)
        now["highest"] = jnp.maximum(now["highest"], peak)

    def take_weights(now, step):
        source, part = now["tile"] + step, now["part"]
        at = slice(step * TILE, (step + 1) * TILE)
        shift = now["highest"] * factor
        off = shift if valid[source] is None else jnp.where(valid[source], shift, jnp.inf)
        weight = jnp.exp2(weights[part, at, :] * factor - off)
        weights[part, at, :] = weight
        now["total"] = now["total"] + jnp.sum(weight, axis=0, keepdims=True)

    def take_shares(now, step):
        source, part = now["tile"] + step, now["part"]
        if step == 0:
            now["inverse"] = 1.0 / now["total"]
        rounded = (weights[part, step * TILE : (step + 1) * TILE, :] * now["inverse"]).astype(jnp.bfloat16)
        shares_out[source * TILE : (source + 1) * TILE, part * TILE : (part + 1) * TILE] = rounded
        if step == 4:
            span = slice(now["tile"] * TILE, (now["tile"] + 5) * TILE)
            now["attended"] = product(value_cols[:, span], shares_out[span, part * TILE : (part + 1) * TILE], NN)

    def take_grads(now, step):
        source, part = now["tile"] + step, now["part"]
        if step == 0:
            now["row_dot"] = jnp.sum(now["attended"] * all_grad_cols[now["columns"], now["rows"]], axis=0, keepdims=True)
        share_grad = product(value_rows[source * TILE : (source + 1) * TILE, :], grads[now["rows"], now["columns"]], NT)
        share = weights[part, step * TILE : (step + 1) * TILE, :] * now["inverse"]
        score_grad = (share * (share_grad - now["row_dot"])).astype(jnp.bfloat16)
        score_out[source * TILE : (source + 1) * TILE, part * TILE : (part + 1) * TILE] = score_grad
        if step == 4:
            span = slice(now["tile"] * TILE, (now["tile"] + 5) * TILE)
            now["query_part"] = product(key_cols[:, span], score_out[span, part * TILE : (part + 1) * TILE], NN)
            query_grad[now["rows"], now["member"] * HEAD_SIZE : (now["member"] + 1) * HEAD_SIZE] = (
                (now["query_part"] * scale).T.astype(jnp.bfloat16)
            )

    stages = (take_grads, take_shares, take_weights, take_scores)
    for turn in range(len(parts) + len(stages) - 1):
        for step in range(5):
            for stage, take in enumerate(stages):
                at = turn - (len(stages) - 1 - stage)
                if 0 <= at < len(parts):
                    take(parts[at], step)

    for source in range(6):
        rows = slice(source * TILE, (source + 1) * TILE)
        out, first = ((grad2, 0), (grad1, 2), (grad0, 4))[source // 2]
        target = slice((source - first) * TILE, (source - first + 1) * TILE)
        lanes_of = [slice((2 * head + member) * HEAD_SIZE, (2 * head + member + 1) * HEAD_SIZE) for member in range(2)]
        if 1 <= source <= 4:
            query_rows = slice(0, BLOCK)
            left = (score_out[rows, :], shares_out[rows, :])
        else:
            tile = 0 if source == 0 else 1
            query_rows = slice(tile * TILE, (tile + 1) * TILE)
            left = [
                jnp.concatenate([kept[rows, (2 * member + tile) * TILE : (2 * member + tile + 1) * TILE] for member in range(2)], axis=1)
                for kept in (score_out, shares_out)
            ]
        key_part = product(left[0], jnp.concatenate([queries[query_rows, lanes] for lanes in lanes_of], axis=0), NN)
        value_part = product(left[1], jnp.concatenate([grads[query_rows, lanes] for lanes in lanes_of], axis=0), NN)
        out[target, 0:HEAD_SIZE] = (key_part * scale).astype(out.dtype)
        out[target, HEAD_SIZE : 2 * HEAD_SIZE] = value_part.astype(out.dtype)


def attend_call(head, *operands):
    return vmem_call(
        functools.partial(attend_kernel, head),
        (shape_of(BLOCK, 256), shape_of(BLOCK, 256, jnp.float32), shape_of(BLOCK, 256), shape_of(BLOCK, 256, jnp.float32)),
        operands,
        in_specs=[SMEM] + [VMEM] * 8,
        mebibytes=18,
        scratch=[
            pltpu.VMEM((WINDOW_ROWS, HEAD_SIZE), jnp.bfloat16),
            pltpu.VMEM((WINDOW_ROWS, HEAD_SIZE), jnp.bfloat16),
            pltpu.VMEM((HEAD_SIZE, WINDOW_ROWS), jnp.bfloat16),
            pltpu.VMEM((HEAD_SIZE, WINDOW_ROWS), jnp.bfloat16),
            pltpu.VMEM((4, 5 * TILE, TILE), jnp.float32),
            pltpu.VMEM((WINDOW_ROWS, 4 * TILE), jnp.bfloat16),
            pltpu.VMEM((WINDOW_ROWS, 4 * TILE), jnp.bfloat16),
        ],
    )


def merge_kernel(place, older, arrived, out):
    odd = (place[0] & 1).astype(jnp.float32)
    out[...] = (older[...] + odd * arrived[...].astype(jnp.float32)).astype(jnp.bfloat16)


def finish_kernel(head, place, key_exps, value_exps, own, sibling, later, out):
    even = (1 - (place[0] & 1)).astype(jnp.float32)
    for block in range(BLOCK // SCALE_BLOCK):
        rows = slice(block * SCALE_BLOCK, (block + 1) * SCALE_BLOCK)
        for part, exponents in ((0, key_exps), (1, value_exps)):
            at = (rows, slice(part * HEAD_SIZE, (part + 1) * HEAD_SIZE))
            total = own[at] + even * sibling[at].astype(jnp.float32) + later[at].astype(jnp.float32)
            out[at] = (total * factor_of(exponents[head, block])).astype(jnp.bfloat16)


def remote_part(place, head, half_at, pieces, mine, other):
    half = HALF_ROWS
    lanes = slice(head * HEAD_SIZE, (head + 1) * HEAD_SIZE)
    parts = []
    for matrix in mine if half_at == 0 else other:
        parts += [matrix[0:half, lanes], matrix[half : 2 * half, lanes]]
    return product(jnp.concatenate(parts, axis=1), jnp.concatenate([piece[...] for piece in pieces], axis=1), NT)


def half_slice(place, half_at):
    core = place[0] & 1
    at = core if half_at == 0 else 1 - core
    return pl.ds(pl.multiple_of(at * HALF_ROWS, 16), HALF_ROWS)


def early_kernel(place, group, keys, values, own0, own1, *rest):
    pieces, mine, other, out, rows, arrivals = rest[:3], rest[3:6], rest[6:9], rest[9], rest[10], rest[11]
    begin = pl.multiple_of(group[0] * (2 * HALF_ROWS), 16)
    copies = [
        pltpu.make_async_copy(matrix.at[pl.ds(begin, 2 * HALF_ROWS), :], rows.at[part], arrivals.at[part])
        for part, matrix in enumerate((keys, values))
    ]
    for copy in copies:
        copy.start()
    for half_at in range(2):
        out[half_slice(place, half_at), :] = remote_part(place, 0, half_at, pieces, mine, other)
    for copy in copies:
        copy.wait()
    channels = jnp.concatenate(
        [own0[:, :HEAD_SIZE], own1[:, :HEAD_SIZE], own0[:, HEAD_SIZE:], own1[:, HEAD_SIZE:]], axis=1
    )
    for half_at in range(2):
        at = slice(half_at * HALF_ROWS, (half_at + 1) * HALF_ROWS)
        out[at, :] += product(jnp.concatenate([rows[0, at, :], rows[1, at, :]], axis=1), channels, NT)


def late_kernel(place, early, *rest):
    pieces, mine, other, out = rest[:3], rest[3:6], rest[6:9], rest[9]
    for half_at in range(2):
        rows = half_slice(place, half_at)
        out[rows, :] = (early[rows, :] + remote_part(place, 1, half_at, pieces, mine, other)).astype(out.dtype)


def prepare_kernel(queries, grads, ready, query_out, grad_out, grad_cols):
    query_out[...] = queries[...]
    grad_out[...] = grads[...]
    eye = identity()
    for head in range(4):
        lanes = slice(head * HEAD_SIZE, (head + 1) * HEAD_SIZE)
        grad_cols[lanes, :] = product(eye, grads[:, lanes], NT)


def shift_pairs(count, steps):
    return [(at, at + steps) for at in range(max(0, -steps), min(count, count - steps))]


def local(
    queries, keys, values, output_gradient, key_exponents, value_exponents, key_matrix, value_matrix
):
    count = lax.axis_size("seq")
    groups = lax.axis_size("head")
    index = lax.axis_index("seq")
    place = index.astype(jnp.int32).reshape(1)
    group = lax.axis_index("head").astype(jnp.int32).reshape(1)
    core = index & 1
    siblings = [(at, at ^ 1) for at in range(count)]

    def to_sibling(value):
        return lax.ppermute(value, "seq", siblings)

    def onward(value, steps):
        return lax.ppermute(value, "seq", shift_pairs(count, steps))

    key_exponents, value_exponents = key_exponents.T, value_exponents.T
    model_rows = key_matrix.shape[0] // groups
    piece_shape = shape_of(model_rows, 256)
    exact_keys, exact_values, key_total = vmem_call(
        dequantize_kernel,
        (shape_of(BLOCK, 256), shape_of(BLOCK, 256), shape_of(8, 256, jnp.float32)),
        (key_exponents, value_exponents, keys, values),
        in_specs=[SMEM, SMEM, VMEM, VMEM],
    )
    older_keys = onward(exact_keys, 2)
    last_total = onward(key_total, 1)

    def along_head(value, steps):
        return lax.ppermute(value, "head", [(at, (at + steps) % groups) for at in range(groups)])


    older_values = onward(exact_values, 2)
    smooth = vmem_call(
        smooth_kernel, shape_of(BLOCK, 256), (place, exact_keys, older_keys, last_total), in_specs=[SMEM, VMEM, VMEM, VMEM]
    )
    older_smooth = onward(smooth, 2)
    sent = pl.pallas_call(
        cut_kernel,
        out_shape=(piece_shape,) * 3,
        in_specs=[SMEM, SMEM, HBM, HBM, pl.BlockSpec(memory_space=pl.ANY)],
        out_specs=(HBM,) * 3,
        scratch_shapes=[
            pltpu.VMEM((3, model_rows, 256), jnp.bfloat16),
            pltpu.SemaphoreType.DMA((6,)),
            pltpu.SemaphoreType.DMA((3,)),
        ],
        cost_estimate=pl.CostEstimate(flops=1, bytes_accessed=1, transcendentals=0),
        compiler_params=pltpu.CompilerParams(vmem_limit_bytes=CUT_LIMIT * MEBI),
    )(place, group, key_matrix, value_matrix, smooth)
    fetched = [along_head(piece, steps) for steps, piece in zip((1, 2, 3), sent)]
    last = to_sibling(
        jnp.where(
            core == 0,
            jnp.concatenate([smooth, exact_values], axis=1),
            jnp.concatenate([older_smooth, older_values], axis=1),
        )
    )

    queries, output_gradient, grad_cols = vmem_call(
        prepare_kernel,
        (shape_of(BLOCK, 512), shape_of(BLOCK, 512), shape_of(512, BLOCK, jnp.float32)),
        (queries, output_gradient, smooth),
        in_specs=[VMEM, VMEM, pl.BlockSpec(memory_space=pl.ANY)],
    )

    query_grads, gathered = [], []
    for head in range(2):
        if head == 1:
            queries, _, swapped[0], swapped[2] = lax.optimization_barrier((queries, back, swapped[0], swapped[2]))
        query_part, grad2, grad1, grad0 = attend_call(
            head, place, queries, output_gradient, grad_cols, older_smooth, last, smooth, older_values, exact_values
        )
        query_grads.append(query_part)
        if head == 0:
            fetched[0], fetched[2], _ = lax.optimization_barrier((fetched[0], fetched[2], grad1))
            swapped = [to_sibling(fetched[0]), None, to_sibling(fetched[2])]
        sibling_grad = to_sibling(grad1)
        if head == 1:
            grad2, _ = lax.optimization_barrier((grad2, gathered[0][0]))
        back = vmem_call(merge_kernel, shape_of(BLOCK, 256), (place, grad2, sibling_grad), in_specs=[SMEM, VMEM, VMEM])
        later_grad = onward(back, -2)
        scaled = vmem_call(
            functools.partial(finish_kernel, head),
            shape_of(BLOCK, 256),
            (place, key_exponents, value_exponents, grad0, sibling_grad, later_grad),
            in_specs=[SMEM, SMEM, SMEM, VMEM, VMEM, VMEM],
        )
        arrived = [scaled]
        for steps in (1, 2, 3):
            arrived.append(along_head(scaled, steps))
        gathered.append(arrived)
    fetched[1], _ = lax.optimization_barrier((fetched[1], back))
    swapped[1] = to_sibling(fetched[1])
    early = vmem_call(
        early_kernel,
        shape_of(model_rows, BLOCK, jnp.float32),
        (place, group, key_matrix, value_matrix, gathered[0][0], gathered[1][0], *gathered[0][1:], *fetched, *swapped),
        in_specs=[SMEM, SMEM, HBM, HBM] + [VMEM] * 11,
        scratch=[pltpu.VMEM((2, model_rows, 256), jnp.bfloat16), pltpu.SemaphoreType.DMA((2,))],
        mebibytes=18,
    )
    input_grad = vmem_call(
        late_kernel,
        shape_of(model_rows, BLOCK),
        (place, early, *gathered[1][1:], *fetched, *swapped),
        in_specs=[SMEM] + [VMEM] * 10,
        mebibytes=18,
    )
    return jnp.concatenate(query_grads, axis=1), input_grad


def solution(mesh):
    in_specs = (
        P("seq", "head"),
        P("seq", "head"),
        P("seq", "head"),
        P("seq", "head"),
        P("seq", "head"),
        P("seq", "head"),
        P(None, "head"),
        P(None, "head"),
    )
    out_specs = (P("seq", "head"), P("head", "seq"))
    return jax.shard_map(local, mesh=mesh, in_specs=in_specs, out_specs=out_specs, check_vma=False)
```

```python
import functools

import jax
import jax.numpy as jnp
from jax import lax
from jax.experimental import pallas as pl
from jax.experimental.pallas import tpu as pltpu
from jax.sharding import PartitionSpec as P

HEAD_SIZE = 128
QUERY_SCALE = 168
ATTEND_WINDOW = 1024
SCALE_BLOCK = 128
TILE = 256
BLOCK = 512
WINDOW_ROWS = 3 * BLOCK
HALF_ROWS = 672
LOG2_E = 1.4426950408889634
MEBI = 1024 * 1024
CUT_LIMIT = 57

NN = (((1,), (0,)), ((), ()))
NT = (((1,), (1,)), ((), ()))


def product(left, right, dims):
    return lax.dot_general(left, right, dims, preferred_element_type=jnp.float32)


def vmem_call(kernel, out_shapes, inputs, in_specs=None, scratch=(), mebibytes=8, flops=1):
    whole = pl.BlockSpec(memory_space=pltpu.VMEM)
    return pl.pallas_call(
        kernel,
        out_shape=out_shapes,
        in_specs=in_specs if in_specs is not None else [whole] * len(inputs),
        out_specs=jax.tree.map(lambda _: whole, out_shapes),
        scratch_shapes=list(scratch),
        cost_estimate=pl.CostEstimate(flops=flops, bytes_accessed=1, transcendentals=0),
        compiler_params=pltpu.CompilerParams(vmem_limit_bytes=mebibytes * MEBI),
    )(*inputs)


def shape_of(rows, columns, dtype=jnp.bfloat16):
    return jax.ShapeDtypeStruct((rows, columns), dtype)


SMEM = pl.BlockSpec(memory_space=pltpu.SMEM)
VMEM = pl.BlockSpec(memory_space=pltpu.VMEM)
HBM = pl.BlockSpec(memory_space=pltpu.MemorySpace.HBM)


def factor_of(exponent):
    return jnp.where(exponent > 0, 2.0, jnp.where(exponent < 0, 0.5, 1.0)).astype(jnp.float32)


def identity():
    row = lax.broadcasted_iota(jnp.int32, (HEAD_SIZE, HEAD_SIZE), 0)
    column = lax.broadcasted_iota(jnp.int32, (HEAD_SIZE, HEAD_SIZE), 1)
    return (row == column).astype(jnp.float32).astype(jnp.bfloat16)


def dequantize_kernel(key_exps, value_exps, keys, values, key_out, value_out, total_out):
    for part, (source, exponents, target) in enumerate(((keys, key_exps, key_out), (values, value_exps, value_out))):
        for head in range(2):
            lanes = slice(head * HEAD_SIZE, (head + 1) * HEAD_SIZE)
            total = jnp.zeros((1, HEAD_SIZE), jnp.float32)
            for block in range(BLOCK // SCALE_BLOCK):
                rows = slice(block * SCALE_BLOCK, (block + 1) * SCALE_BLOCK)
                scaled = source[rows, lanes].astype(jnp.float32) * factor_of(exponents[head, block])
                target[rows, lanes] = scaled.astype(jnp.bfloat16)
                if part == 0:
                    total = total + jnp.sum(scaled, axis=0, keepdims=True)
            if part == 0:
                total_out[:, lanes] = jnp.broadcast_to(total, (8, HEAD_SIZE))


def cut_kernel(index, group, key_matrix, value_matrix, ready, near, far, near_rows, far_rows, arrivals, departures):
    half = HALF_ROWS
    core = index[0] & 1
    begins = (
        pl.multiple_of(((group[0] + 1 + 2 * core) & 3) * (2 * half), 16),
        pl.multiple_of(((group[0] + 2) & 3) * (2 * half) + core * half, 16),
    )
    incoming, outgoing = [], []
    for at, (begin, count, kept, target) in enumerate(
        ((begins[0], 2 * half, near_rows, near), (begins[1], half, far_rows, far))
    ):
        for part, matrix in enumerate((key_matrix, value_matrix)):
            incoming.append(
                pltpu.make_async_copy(
                    matrix.at[pl.ds(begin, count), :], kept.at[pl.ds(part * count, count), :], arrivals.at[2 * at + part]
                )
            )
        outgoing.append(pltpu.make_async_copy(kept, target, departures.at[at]))
    for copy in incoming:
        copy.start()
    for at in range(2):
        incoming[2 * at].wait()
        incoming[2 * at + 1].wait()
        outgoing[at].start()
    for copy in outgoing:
        copy.wait()


def smooth_kernel(place, own, older, total, smooth_out):
    first = place[0] * BLOCK
    row = lax.broadcasted_iota(jnp.int32, (BLOCK, BLOCK), 0)
    column = lax.broadcasted_iota(jnp.int32, (BLOCK, BLOCK), 1)
    upto = (column <= row).astype(jnp.float32).astype(jnp.bfloat16)
    after = (column > row).astype(jnp.float32).astype(jnp.bfloat16)
    sums = product(upto, own[...], NN) + product(after, older[...], NN) + total[0:1, :]
    position = first + lax.broadcasted_iota(jnp.int32, (BLOCK, 1), 0)
    counts = jnp.minimum(position + 1, ATTEND_WINDOW).astype(jnp.float32)
    smooth_out[...] = (own[...].astype(jnp.float32) - sums / counts).astype(jnp.bfloat16)


def attend_kernel(
    head, place, queries, grads, all_grad_cols, keys2, last, keys0, values2, values0,
    query_grad, grad2, grad1, grad0,
    key_rows, value_rows, key_cols, value_cols, weights, shares_out, score_out,
):
    scale = QUERY_SCALE ** (-0.5)
    index = place[0]
    lanes = slice(head * HEAD_SIZE, (head + 1) * HEAD_SIZE)
    last_lanes = slice(256 + head * HEAD_SIZE, 256 + (head + 1) * HEAD_SIZE)
    for at, source in enumerate((keys2, last, keys0)):
        key_rows[at * BLOCK : (at + 1) * BLOCK, :] = source[:, lanes]
    for at, source in enumerate((values2, last, values0)):
        value_rows[at * BLOCK : (at + 1) * BLOCK, :] = source[:, last_lanes if at == 1 else lanes]
    eye = identity()
    key_cols[...] = product(eye, key_rows[...], NT).astype(jnp.bfloat16)
    value_cols[...] = product(eye, value_rows[...], NT).astype(jnp.bfloat16)
    key_at = lax.broadcasted_iota(jnp.int32, (TILE, TILE), 0)
    query_at = lax.broadcasted_iota(jnp.int32, (TILE, TILE), 1)
    lowest = -jnp.inf

    valid = [index >= 2, index >= 2, index >= 1, index >= 1, None, None]
    factor = scale * LOG2_E
    parts = []
    for tile in range(BLOCK // TILE):
        for member in range(2):
            part = 2 * member + tile
            rows = slice(tile * TILE, (tile + 1) * TILE)
            columns = slice((2 * head + member) * HEAD_SIZE, (2 * head + member + 1) * HEAD_SIZE)
            parts.append(dict(
                part=part, tile=tile, member=member, rows=rows, columns=columns,
                highest=jnp.full((1, TILE), lowest, jnp.float32),
                total=jnp.zeros((1, TILE), jnp.float32),
                attended=jnp.zeros((HEAD_SIZE, TILE), jnp.float32),
                query_part=jnp.zeros((HEAD_SIZE, TILE), jnp.float32),
            ))

    def take_scores(now, step):
        source, part = now["tile"] + step, now["part"]
        scores = product(key_rows[source * TILE : (source + 1) * TILE, :], queries[now["rows"], now["columns"]], NT)
        if step == 0:
            scores = jnp.where(key_at > query_at, scores, lowest)
        if step == 4:
            scores = jnp.where(key_at <= query_at, scores, lowest)
        weights[part, step * TILE : (step + 1) * TILE, :] = scores
        peak = jnp.max(scores, axis=0, keepdims=True)
        if valid[source] is not None:
            peak = jnp.where(valid[source], peak, lowest)
        now["highest"] = jnp.maximum(now["highest"], peak)

    def take_weights(now, step):
        source, part = now["tile"] + step, now["part"]
        at = slice(step * TILE, (step + 1) * TILE)
        shift = now["highest"] * factor
        off = shift if valid[source] is None else jnp.where(valid[source], shift, jnp.inf)
        weight = jnp.exp2(weights[part, at, :] * factor - off)
        weights[part, at, :] = weight
        now["total"] = now["total"] + jnp.sum(weight, axis=0, keepdims=True)

    def take_shares(now, step):
        source, part = now["tile"] + step, now["part"]
        if step == 0:
            now["inverse"] = 1.0 / now["total"]
        rounded = (weights[part, step * TILE : (step + 1) * TILE, :] * now["inverse"]).astype(jnp.bfloat16)
        shares_out[source * TILE : (source + 1) * TILE, part * TILE : (part + 1) * TILE] = rounded
        if step == 4:
            span = slice(now["tile"] * TILE, (now["tile"] + 5) * TILE)
            now["attended"] = product(value_cols[:, span], shares_out[span, part * TILE : (part + 1) * TILE], NN)

    def take_grads(now, step):
        source, part = now["tile"] + step, now["part"]
        if step == 0:
            now["row_dot"] = jnp.sum(now["attended"] * all_grad_cols[now["columns"], now["rows"]], axis=0, keepdims=True)
        share_grad = product(value_rows[source * TILE : (source + 1) * TILE, :], grads[now["rows"], now["columns"]], NT)
        share = weights[part, step * TILE : (step + 1) * TILE, :] * now["inverse"]
        score_grad = (share * (share_grad - now["row_dot"])).astype(jnp.bfloat16)
        score_out[source * TILE : (source + 1) * TILE, part * TILE : (part + 1) * TILE] = score_grad
        if step == 4:
            span = slice(now["tile"] * TILE, (now["tile"] + 5) * TILE)
            now["query_part"] = product(key_cols[:, span], score_out[span, part * TILE : (part + 1) * TILE], NN)
            query_grad[now["rows"], now["member"] * HEAD_SIZE : (now["member"] + 1) * HEAD_SIZE] = (
                (now["query_part"] * scale).T.astype(jnp.bfloat16)
            )

    stages = (take_grads, take_shares, take_weights, take_scores)
    for turn in range(len(parts) + len(stages) - 1):
        for step in range(5):
            for stage, take in enumerate(stages):
                at = turn - (len(stages) - 1 - stage)
                if 0 <= at < len(parts):
                    take(parts[at], step)

    for source in range(6):
        rows = slice(source * TILE, (source + 1) * TILE)
        out, first = ((grad2, 0), (grad1, 2), (grad0, 4))[source // 2]
        target = slice((source - first) * TILE, (source - first + 1) * TILE)
        lanes_of = [slice((2 * head + member) * HEAD_SIZE, (2 * head + member + 1) * HEAD_SIZE) for member in range(2)]
        if 1 <= source <= 4:
            query_rows = slice(0, BLOCK)
            left = (score_out[rows, :], shares_out[rows, :])
        else:
            tile = 0 if source == 0 else 1
            query_rows = slice(tile * TILE, (tile + 1) * TILE)
            left = [
                jnp.concatenate([kept[rows, (2 * member + tile) * TILE : (2 * member + tile + 1) * TILE] for member in range(2)], axis=1)
                for kept in (score_out, shares_out)
            ]
        key_part = product(left[0], jnp.concatenate([queries[query_rows, lanes] for lanes in lanes_of], axis=0), NN)
        value_part = product(left[1], jnp.concatenate([grads[query_rows, lanes] for lanes in lanes_of], axis=0), NN)
        out[target, 0:HEAD_SIZE] = (key_part * scale).astype(out.dtype)
        out[target, HEAD_SIZE : 2 * HEAD_SIZE] = value_part.astype(out.dtype)


def attend_call(head, *operands):
    return vmem_call(
        functools.partial(attend_kernel, head),
        (shape_of(BLOCK, 256), shape_of(BLOCK, 256, jnp.float32), shape_of(BLOCK, 256), shape_of(BLOCK, 256, jnp.float32)),
        operands,
        in_specs=[SMEM] + [VMEM] * 8,
        mebibytes=18,
        scratch=[
            pltpu.VMEM((WINDOW_ROWS, HEAD_SIZE), jnp.bfloat16),
            pltpu.VMEM((WINDOW_ROWS, HEAD_SIZE), jnp.bfloat16),
            pltpu.VMEM((HEAD_SIZE, WINDOW_ROWS), jnp.bfloat16),
            pltpu.VMEM((HEAD_SIZE, WINDOW_ROWS), jnp.bfloat16),
            pltpu.VMEM((4, 5 * TILE, TILE), jnp.float32),
            pltpu.VMEM((WINDOW_ROWS, 4 * TILE), jnp.bfloat16),
            pltpu.VMEM((WINDOW_ROWS, 4 * TILE), jnp.bfloat16),
        ],
    )


def merge_kernel(place, older, arrived, out):
    odd = (place[0] & 1).astype(jnp.float32)
    out[...] = (older[...] + odd * arrived[...].astype(jnp.float32)).astype(jnp.bfloat16)


def finish_kernel(head, place, key_exps, value_exps, own, sibling, later, out):
    even = (1 - (place[0] & 1)).astype(jnp.float32)
    for block in range(BLOCK // SCALE_BLOCK):
        rows = slice(block * SCALE_BLOCK, (block + 1) * SCALE_BLOCK)
        for part, exponents in ((0, key_exps), (1, value_exps)):
            at = (rows, slice(part * HEAD_SIZE, (part + 1) * HEAD_SIZE))
            total = own[at] + even * sibling[at].astype(jnp.float32) + later[at].astype(jnp.float32)
            out[at] = (total * factor_of(exponents[head, block])).astype(jnp.bfloat16)


def remote_parts(place, head, pieces, matrices):
    before, opposite, after = pieces
    near, other_near, far, other_far = matrices
    half = HALF_ROWS
    core = place[0] & 1
    even = jnp.broadcast_to(core == 0, before.shape)
    lanes = slice(head * HEAD_SIZE, (head + 1) * HEAD_SIZE)
    first, second = before[...].astype(jnp.float32), after[...].astype(jnp.float32)
    channels = jnp.concatenate(
        [
            jnp.where(even, first, second).astype(jnp.bfloat16),
            jnp.where(even, second, first).astype(jnp.bfloat16),
            opposite[...],
        ],
        axis=1,
    )
    for at, opposite_rows in ((core, far), (1 - core, other_far)):
        begin = pl.multiple_of(at * half, 16)
        parts = []
        for matrix in (near, other_near):
            for part in range(2):
                parts.append(matrix[pl.ds(pl.multiple_of(part * 2 * half + begin, 16), half), lanes])
        parts += [opposite_rows[0:half, lanes], opposite_rows[half : 2 * half, lanes]]
        yield pl.ds(begin, half), product(jnp.concatenate(parts, axis=1), channels, NT)


def early_kernel(place, group, keys, values, own0, own1, *rest):
    pieces, matrices, out, rows, arrivals = rest[:3], rest[3:7], rest[7], rest[8], rest[9]
    begin = pl.multiple_of(group[0] * (2 * HALF_ROWS), 16)
    copies = [
        pltpu.make_async_copy(matrix.at[pl.ds(begin, 2 * HALF_ROWS), :], rows.at[part], arrivals.at[part])
        for part, matrix in enumerate((keys, values))
    ]
    for copy in copies:
        copy.start()
    for at, part in remote_parts(place, 0, pieces, matrices):
        out[at, :] = part
    for copy in copies:
        copy.wait()
    channels = jnp.concatenate(
        [own0[:, :HEAD_SIZE], own1[:, :HEAD_SIZE], own0[:, HEAD_SIZE:], own1[:, HEAD_SIZE:]], axis=1
    )
    for half_at in range(2):
        at = slice(half_at * HALF_ROWS, (half_at + 1) * HALF_ROWS)
        out[at, :] += product(jnp.concatenate([rows[0, at, :], rows[1, at, :]], axis=1), channels, NT)


def late_kernel(place, early, *rest):
    pieces, matrices, out = rest[:3], rest[3:7], rest[7]
    for at, part in remote_parts(place, 1, pieces, matrices):
        out[at, :] = (early[at, :] + part).astype(out.dtype)


def prepare_kernel(queries, grads, ready, query_out, grad_out, grad_cols):
    query_out[...] = queries[...]
    grad_out[...] = grads[...]
    eye = identity()
    for head in range(4):
        lanes = slice(head * HEAD_SIZE, (head + 1) * HEAD_SIZE)
        grad_cols[lanes, :] = product(eye, grads[:, lanes], NT)


def shift_pairs(count, steps):
    return [(at, at + steps) for at in range(max(0, -steps), min(count, count - steps))]


def local(
    queries, keys, values, output_gradient, key_exponents, value_exponents, key_matrix, value_matrix
):
    count = lax.axis_size("seq")
    groups = lax.axis_size("head")
    index = lax.axis_index("seq")
    place = index.astype(jnp.int32).reshape(1)
    group = lax.axis_index("head").astype(jnp.int32).reshape(1)
    core = index & 1
    siblings = [(at, at ^ 1) for at in range(count)]

    def to_sibling(value):
        return lax.ppermute(value, "seq", siblings)

    def onward(value, steps):
        return lax.ppermute(value, "seq", shift_pairs(count, steps))

    def along_head(value, steps):
        return lax.ppermute(value, "head", [(at, (at + steps) % groups) for at in range(groups)])

    key_exponents, value_exponents = key_exponents.T, value_exponents.T
    model_rows = key_matrix.shape[0] // groups
    exact_keys, exact_values, key_total = vmem_call(
        dequantize_kernel,
        (shape_of(BLOCK, 256), shape_of(BLOCK, 256), shape_of(8, 256, jnp.float32)),
        (key_exponents, value_exponents, keys, values),
        in_specs=[SMEM, SMEM, VMEM, VMEM],
    )
    older_keys = onward(exact_keys, 2)
    last_total = onward(key_total, 1)


    near_sent, far_sent = pl.pallas_call(
        cut_kernel,
        out_shape=(shape_of(2 * model_rows, 256), shape_of(model_rows, 256)),
        in_specs=[SMEM, SMEM, HBM, HBM, pl.BlockSpec(memory_space=pl.ANY)],
        out_specs=(HBM,) * 2,
        scratch_shapes=[
            pltpu.VMEM((2 * model_rows, 256), jnp.bfloat16),
            pltpu.VMEM((model_rows, 256), jnp.bfloat16),
            pltpu.SemaphoreType.DMA((4,)),
            pltpu.SemaphoreType.DMA((2,)),
        ],
        cost_estimate=pl.CostEstimate(flops=1, bytes_accessed=1, transcendentals=0),
        compiler_params=pltpu.CompilerParams(vmem_limit_bytes=CUT_LIMIT * MEBI),
    )(place, group, key_matrix, value_matrix, keys)
    near_pairs = [
        (at * groups + there, at * groups + (there + (1 if at % 2 == 0 else groups - 1)) % groups)
        for at in range(count)
        for there in range(groups)
    ]
    older_values = onward(exact_values, 2)
    smooth = vmem_call(
        smooth_kernel, shape_of(BLOCK, 256), (place, exact_keys, older_keys, last_total), in_specs=[SMEM, VMEM, VMEM, VMEM]
    )
    older_smooth = onward(smooth, 2)
    near = lax.ppermute(near_sent, ("seq", "head"), near_pairs)
    far = along_head(far_sent, 2)

    last = to_sibling(
        jnp.where(
            core == 0,
            jnp.concatenate([smooth, exact_values], axis=1),
            jnp.concatenate([older_smooth, older_values], axis=1),
        )
    )

    queries, output_gradient, grad_cols = vmem_call(
        prepare_kernel,
        (shape_of(BLOCK, 512), shape_of(BLOCK, 512), shape_of(512, BLOCK, jnp.float32)),
        (queries, output_gradient, smooth),
        in_specs=[VMEM, VMEM, pl.BlockSpec(memory_space=pl.ANY)],
    )

    query_grads, gathered = [], []
    for head in range(2):
        if head == 1:
            queries, _, other_near = lax.optimization_barrier((queries, back, other_near))
        query_part, grad2, grad1, grad0 = attend_call(
            head, place, queries, output_gradient, grad_cols, older_smooth, last, smooth, older_values, exact_values
        )
        query_grads.append(query_part)
        if head == 0:
            near_now, far, _ = lax.optimization_barrier((near, far, grad1))
            other_near, other_far = to_sibling(near_now), to_sibling(far)
        sibling_grad = to_sibling(grad1)
        if head == 1:
            grad2, _ = lax.optimization_barrier((grad2, gathered[0][0]))
        back = vmem_call(merge_kernel, shape_of(BLOCK, 256), (place, grad2, sibling_grad), in_specs=[SMEM, VMEM, VMEM])
        later_grad = onward(back, -2)
        scaled = vmem_call(
            functools.partial(finish_kernel, head),
            shape_of(BLOCK, 256),
            (place, key_exponents, value_exponents, grad0, sibling_grad, later_grad),
            in_specs=[SMEM, SMEM, SMEM, VMEM, VMEM, VMEM],
        )
        arrived = [scaled]
        for steps in (1, 2, 3):
            arrived.append(along_head(scaled, steps))
        gathered.append(arrived)
    fetched = (near, other_near, far, other_far)
    early = vmem_call(
        early_kernel,
        shape_of(model_rows, BLOCK, jnp.float32),
        (place, group, key_matrix, value_matrix, gathered[0][0], gathered[1][0], *gathered[0][1:], *fetched),
        in_specs=[SMEM, SMEM, HBM, HBM] + [VMEM] * 9,
        scratch=[pltpu.VMEM((2, model_rows, 256), jnp.bfloat16), pltpu.SemaphoreType.DMA((2,))],
        mebibytes=18,
    )
    input_grad = vmem_call(
        late_kernel,
        shape_of(model_rows, BLOCK),
        (place, early, *gathered[1][1:], *fetched),
        in_specs=[SMEM] + [VMEM] * 8,
        mebibytes=18,
    )
    return jnp.concatenate(query_grads, axis=1), input_grad


def solution(mesh):
    in_specs = (
        P("seq", "head"),
        P("seq", "head"),
        P("seq", "head"),
        P("seq", "head"),
        P("seq", "head"),
        P("seq", "head"),
        P(None, "head"),
        P(None, "head"),
    )
    out_specs = (P("seq", "head"), P("head", "seq"))
    return jax.shard_map(local, mesh=mesh, in_specs=in_specs, out_specs=out_specs, check_vma=False)
```

```python
import functools

import jax
import jax.numpy as jnp
from jax import lax
from jax.experimental import pallas as pl
from jax.experimental.pallas import tpu as pltpu
from jax.sharding import PartitionSpec as P

HEAD_SIZE = 128
QUERY_SCALE = 168
ATTEND_WINDOW = 1024
SCALE_BLOCK = 128
TILE = 256
BLOCK = 512
WINDOW_ROWS = 3 * BLOCK
HALF_ROWS = 672
LOG2_E = 1.4426950408889634
MEBI = 1024 * 1024
CUT_LIMIT = 57

NN = (((1,), (0,)), ((), ()))
NT = (((1,), (1,)), ((), ()))


def product(left, right, dims):
    return lax.dot_general(left, right, dims, preferred_element_type=jnp.float32)


def vmem_call(kernel, out_shapes, inputs, in_specs=None, scratch=(), mebibytes=8, flops=1):
    whole = pl.BlockSpec(memory_space=pltpu.VMEM)
    return pl.pallas_call(
        kernel,
        out_shape=out_shapes,
        in_specs=in_specs if in_specs is not None else [whole] * len(inputs),
        out_specs=jax.tree.map(lambda _: whole, out_shapes),
        scratch_shapes=list(scratch),
        cost_estimate=pl.CostEstimate(flops=flops, bytes_accessed=1, transcendentals=0),
        compiler_params=pltpu.CompilerParams(vmem_limit_bytes=mebibytes * MEBI),
    )(*inputs)


def shape_of(rows, columns, dtype=jnp.bfloat16):
    return jax.ShapeDtypeStruct((rows, columns), dtype)


SMEM = pl.BlockSpec(memory_space=pltpu.SMEM)
VMEM = pl.BlockSpec(memory_space=pltpu.VMEM)
HBM = pl.BlockSpec(memory_space=pltpu.MemorySpace.HBM)


def factor_of(exponent):
    return jnp.where(exponent > 0, 2.0, jnp.where(exponent < 0, 0.5, 1.0)).astype(jnp.float32)


def identity():
    row = lax.broadcasted_iota(jnp.int32, (HEAD_SIZE, HEAD_SIZE), 0)
    column = lax.broadcasted_iota(jnp.int32, (HEAD_SIZE, HEAD_SIZE), 1)
    return (row == column).astype(jnp.float32).astype(jnp.bfloat16)


def dequantize_kernel(key_exps, value_exps, keys, values, key_out, value_out, total_out):
    for part, (source, exponents, target) in enumerate(((keys, key_exps, key_out), (values, value_exps, value_out))):
        for head in range(2):
            lanes = slice(head * HEAD_SIZE, (head + 1) * HEAD_SIZE)
            total = jnp.zeros((1, HEAD_SIZE), jnp.float32)
            for block in range(BLOCK // SCALE_BLOCK):
                rows = slice(block * SCALE_BLOCK, (block + 1) * SCALE_BLOCK)
                scaled = source[rows, lanes].astype(jnp.float32) * factor_of(exponents[head, block])
                target[rows, lanes] = scaled.astype(jnp.bfloat16)
                if part == 0:
                    total = total + jnp.sum(scaled, axis=0, keepdims=True)
            if part == 0:
                total_out[:, lanes] = jnp.broadcast_to(total, (8, HEAD_SIZE))


def cut_kernel(index, group, key_matrix, value_matrix, ready, near, far, near_rows, far_rows, arrivals, departures):
    half = HALF_ROWS
    core = index[0] & 1
    begins = (
        pl.multiple_of(((group[0] + 1 + 2 * core) & 3) * (2 * half), 16),
        pl.multiple_of(((group[0] + 2) & 3) * (2 * half) + core * half, 16),
    )
    incoming, outgoing = [], []
    for at, (begin, count, kept, target) in enumerate(
        ((begins[0], 2 * half, near_rows, near), (begins[1], half, far_rows, far))
    ):
        for part, matrix in enumerate((key_matrix, value_matrix)):
            incoming.append(
                pltpu.make_async_copy(
                    matrix.at[pl.ds(begin, count), :], kept.at[pl.ds(part * count, count), :], arrivals.at[2 * at + part]
                )
            )
        outgoing.append(pltpu.make_async_copy(kept, target, departures.at[at]))
    for copy in incoming:
        copy.start()
    for at in range(2):
        incoming[2 * at].wait()
        incoming[2 * at + 1].wait()
        outgoing[at].start()
    for copy in outgoing:
        copy.wait()


def smooth_kernel(place, own, older, total, smooth_out):
    first = place[0] * BLOCK
    row = lax.broadcasted_iota(jnp.int32, (BLOCK, BLOCK), 0)
    column = lax.broadcasted_iota(jnp.int32, (BLOCK, BLOCK), 1)
    upto = (column <= row).astype(jnp.float32).astype(jnp.bfloat16)
    after = (column > row).astype(jnp.float32).astype(jnp.bfloat16)
    sums = product(upto, own[...], NN) + product(after, older[...], NN) + total[0:1, :]
    position = first + lax.broadcasted_iota(jnp.int32, (BLOCK, 1), 0)
    counts = jnp.minimum(position + 1, ATTEND_WINDOW).astype(jnp.float32)
    smooth_out[...] = (own[...].astype(jnp.float32) - sums / counts).astype(jnp.bfloat16)


def attend_kernel(
    head, place, queries, grads, all_grad_cols, keys2, last, keys0, values2, values0,
    query_grad, grad2, grad1, grad0,
    key_rows, value_rows, key_cols, value_cols, weights, shares_out, score_out,
):
    scale = QUERY_SCALE ** (-0.5)
    index = place[0]
    lanes = slice(head * HEAD_SIZE, (head + 1) * HEAD_SIZE)
    last_lanes = slice(256 + head * HEAD_SIZE, 256 + (head + 1) * HEAD_SIZE)
    for at, source in enumerate((keys2, last, keys0)):
        key_rows[at * BLOCK : (at + 1) * BLOCK, :] = source[:, lanes]
    for at, source in enumerate((values2, last, values0)):
        value_rows[at * BLOCK : (at + 1) * BLOCK, :] = source[:, last_lanes if at == 1 else lanes]
    eye = identity()
    key_cols[...] = product(eye, key_rows[...], NT).astype(jnp.bfloat16)
    value_cols[...] = product(eye, value_rows[...], NT).astype(jnp.bfloat16)
    key_at = lax.broadcasted_iota(jnp.int32, (TILE, TILE), 0)
    query_at = lax.broadcasted_iota(jnp.int32, (TILE, TILE), 1)
    lowest = -jnp.inf

    valid = [index >= 2, index >= 2, index >= 1, index >= 1, None, None]
    factor = scale * LOG2_E
    parts = []
    for tile in range(BLOCK // TILE):
        for member in range(2):
            part = 2 * member + tile
            rows = slice(tile * TILE, (tile + 1) * TILE)
            columns = slice((2 * head + member) * HEAD_SIZE, (2 * head + member + 1) * HEAD_SIZE)
            parts.append(dict(
                part=part, tile=tile, member=member, rows=rows, columns=columns,
                highest=jnp.full((1, TILE), lowest, jnp.float32),
                total=jnp.zeros((1, TILE), jnp.float32),
                attended=jnp.zeros((HEAD_SIZE, TILE), jnp.float32),
                query_part=jnp.zeros((HEAD_SIZE, TILE), jnp.float32),
            ))

    def take_scores(now, step):
        source, part = now["tile"] + step, now["part"]
        scores = product(key_rows[source * TILE : (source + 1) * TILE, :], queries[now["rows"], now["columns"]], NT)
        if step == 0:
            scores = jnp.where(key_at > query_at, scores, lowest)
        if step == 4:
            scores = jnp.where(key_at <= query_at, scores, lowest)
        weights[part, step * TILE : (step + 1) * TILE, :] = scores
        peak = jnp.max(scores, axis=0, keepdims=True)
        if valid[source] is not None:
            peak = jnp.where(valid[source], peak, lowest)
        now["highest"] = jnp.maximum(now["highest"], peak)

    def take_weights(now, step):
        source, part = now["tile"] + step, now["part"]
        at = slice(step * TILE, (step + 1) * TILE)
        shift = now["highest"] * factor
        off = shift if valid[source] is None else jnp.where(valid[source], shift, jnp.inf)
        weight = jnp.exp2(weights[part, at, :] * factor - off)
        weights[part, at, :] = weight
        now["total"] = now["total"] + jnp.sum(weight, axis=0, keepdims=True)

    def take_shares(now, step):
        source, part = now["tile"] + step, now["part"]
        if step == 0:
            now["inverse"] = 1.0 / now["total"]
        rounded = (weights[part, step * TILE : (step + 1) * TILE, :] * now["inverse"]).astype(jnp.bfloat16)
        shares_out[source * TILE : (source + 1) * TILE, part * TILE : (part + 1) * TILE] = rounded
        if step == 4:
            span = slice(now["tile"] * TILE, (now["tile"] + 5) * TILE)
            now["attended"] = product(value_cols[:, span], shares_out[span, part * TILE : (part + 1) * TILE], NN)

    def take_grads(now, step):
        source, part = now["tile"] + step, now["part"]
        if step == 0:
            now["row_dot"] = jnp.sum(now["attended"] * all_grad_cols[now["columns"], now["rows"]], axis=0, keepdims=True)
        share_grad = product(value_rows[source * TILE : (source + 1) * TILE, :], grads[now["rows"], now["columns"]], NT)
        share = weights[part, step * TILE : (step + 1) * TILE, :] * now["inverse"]
        score_grad = (share * (share_grad - now["row_dot"])).astype(jnp.bfloat16)
        score_out[source * TILE : (source + 1) * TILE, part * TILE : (part + 1) * TILE] = score_grad
        if step == 4:
            span = slice(now["tile"] * TILE, (now["tile"] + 5) * TILE)
            now["query_part"] = product(key_cols[:, span], score_out[span, part * TILE : (part + 1) * TILE], NN)
            query_grad[now["rows"], now["member"] * HEAD_SIZE : (now["member"] + 1) * HEAD_SIZE] = (
                (now["query_part"] * scale).T.astype(jnp.bfloat16)
            )

    stages = (take_grads, take_shares, take_weights, take_scores)
    for turn in range(len(parts) + len(stages) - 1):
        for step in range(5):
            for stage, take in enumerate(stages):
                at = turn - (len(stages) - 1 - stage)
                if 0 <= at < len(parts):
                    take(parts[at], step)

    for source in range(6):
        rows = slice(source * TILE, (source + 1) * TILE)
        out, first = ((grad2, 0), (grad1, 2), (grad0, 4))[source // 2]
        target = slice((source - first) * TILE, (source - first + 1) * TILE)
        lanes_of = [slice((2 * head + member) * HEAD_SIZE, (2 * head + member + 1) * HEAD_SIZE) for member in range(2)]
        if 1 <= source <= 4:
            query_rows = slice(0, BLOCK)
            left = (score_out[rows, :], shares_out[rows, :])
        else:
            tile = 0 if source == 0 else 1
            query_rows = slice(tile * TILE, (tile + 1) * TILE)
            left = [
                jnp.concatenate([kept[rows, (2 * member + tile) * TILE : (2 * member + tile + 1) * TILE] for member in range(2)], axis=1)
                for kept in (score_out, shares_out)
            ]
        key_part = product(left[0], jnp.concatenate([queries[query_rows, lanes] for lanes in lanes_of], axis=0), NN)
        value_part = product(left[1], jnp.concatenate([grads[query_rows, lanes] for lanes in lanes_of], axis=0), NN)
        out[target, 0:HEAD_SIZE] = (key_part * scale).astype(out.dtype)
        out[target, HEAD_SIZE : 2 * HEAD_SIZE] = value_part.astype(out.dtype)


def attend_call(head, *operands):
    return vmem_call(
        functools.partial(attend_kernel, head),
        (shape_of(BLOCK, 256), shape_of(BLOCK, 256, jnp.float32), shape_of(BLOCK, 256), shape_of(BLOCK, 256, jnp.float32)),
        operands,
        in_specs=[SMEM] + [VMEM] * 8,
        mebibytes=18,
        scratch=[
            pltpu.VMEM((WINDOW_ROWS, HEAD_SIZE), jnp.bfloat16),
            pltpu.VMEM((WINDOW_ROWS, HEAD_SIZE), jnp.bfloat16),
            pltpu.VMEM((HEAD_SIZE, WINDOW_ROWS), jnp.bfloat16),
            pltpu.VMEM((HEAD_SIZE, WINDOW_ROWS), jnp.bfloat16),
            pltpu.VMEM((4, 5 * TILE, TILE), jnp.float32),
            pltpu.VMEM((WINDOW_ROWS, 4 * TILE), jnp.bfloat16),
            pltpu.VMEM((WINDOW_ROWS, 4 * TILE), jnp.bfloat16),
        ],
    )


def merge_kernel(place, older, arrived, out):
    odd = (place[0] & 1).astype(jnp.float32)
    out[...] = (older[...] + odd * arrived[...].astype(jnp.float32)).astype(jnp.bfloat16)


def finish_kernel(head, place, key_exps, value_exps, own, sibling, later, out):
    even = (1 - (place[0] & 1)).astype(jnp.float32)
    for block in range(BLOCK // SCALE_BLOCK):
        rows = slice(block * SCALE_BLOCK, (block + 1) * SCALE_BLOCK)
        for part, exponents in ((0, key_exps), (1, value_exps)):
            at = (rows, slice(part * HEAD_SIZE, (part + 1) * HEAD_SIZE))
            total = own[at] + even * sibling[at].astype(jnp.float32) + later[at].astype(jnp.float32)
            out[at] = (total * factor_of(exponents[head, block])).astype(jnp.bfloat16)


def remote_parts(place, head, pieces, matrices):
    before, opposite, after = pieces
    near, other_near, far, other_far = matrices
    half = HALF_ROWS
    core = place[0] & 1
    even = jnp.broadcast_to(core == 0, before.shape)
    lanes = slice(head * HEAD_SIZE, (head + 1) * HEAD_SIZE)
    first, second = before[...].astype(jnp.float32), after[...].astype(jnp.float32)
    channels = jnp.concatenate(
        [
            jnp.where(even, first, second).astype(jnp.bfloat16),
            jnp.where(even, second, first).astype(jnp.bfloat16),
            opposite[...],
        ],
        axis=1,
    )
    for at, opposite_rows in ((core, far), (1 - core, other_far)):
        begin = pl.multiple_of(at * half, 16)
        parts = []
        for matrix in (near, other_near):
            for part in range(2):
                parts.append(matrix[pl.ds(pl.multiple_of(part * 2 * half + begin, 16), half), lanes])
        parts += [opposite_rows[0:half, lanes], opposite_rows[half : 2 * half, lanes]]
        yield pl.ds(begin, half), product(jnp.concatenate(parts, axis=1), channels, NT)


def early_kernel(place, group, keys, values, own0, own1, *rest):
    pieces, matrices, out, rows, arrivals = rest[:3], rest[3:7], rest[7], rest[8], rest[9]
    begin = pl.multiple_of(group[0] * (2 * HALF_ROWS), 16)
    copies = [
        pltpu.make_async_copy(matrix.at[pl.ds(begin, 2 * HALF_ROWS), :], rows.at[part], arrivals.at[part])
        for part, matrix in enumerate((keys, values))
    ]
    for copy in copies:
        copy.start()
    for at, part in remote_parts(place, 0, pieces, matrices):
        out[at, :] = part
    for copy in copies:
        copy.wait()
    channels = jnp.concatenate(
        [own0[:, :HEAD_SIZE], own1[:, :HEAD_SIZE], own0[:, HEAD_SIZE:], own1[:, HEAD_SIZE:]], axis=1
    )
    for half_at in range(2):
        at = slice(half_at * HALF_ROWS, (half_at + 1) * HALF_ROWS)
        out[at, :] += product(jnp.concatenate([rows[0, at, :], rows[1, at, :]], axis=1), channels, NT)


def late_kernel(place, early, *rest):
    pieces, matrices, out = rest[:3], rest[3:7], rest[7]
    for at, part in remote_parts(place, 1, pieces, matrices):
        out[at, :] = (early[at, :] + part).astype(out.dtype)


def prepare_kernel(queries, grads, ready, query_out, grad_out, grad_cols):
    query_out[...] = queries[...]
    grad_out[...] = grads[...]
    eye = identity()
    for head in range(4):
        lanes = slice(head * HEAD_SIZE, (head + 1) * HEAD_SIZE)
        grad_cols[lanes, :] = product(eye, grads[:, lanes], NT)


def shift_pairs(count, steps):
    return [(at, at + steps) for at in range(max(0, -steps), min(count, count - steps))]


def local(
    queries, keys, values, output_gradient, key_exponents, value_exponents, key_matrix, value_matrix
):
    count = lax.axis_size("seq")
    groups = lax.axis_size("head")
    index = lax.axis_index("seq")
    place = index.astype(jnp.int32).reshape(1)
    group = lax.axis_index("head").astype(jnp.int32).reshape(1)
    core = index & 1
    siblings = [(at, at ^ 1) for at in range(count)]

    def to_sibling(value):
        return lax.ppermute(value, "seq", siblings)

    def onward(value, steps):
        return lax.ppermute(value, "seq", shift_pairs(count, steps))

    def along_head(value, steps):
        return lax.ppermute(value, "head", [(at, (at + steps) % groups) for at in range(groups)])

    key_exponents, value_exponents = key_exponents.T, value_exponents.T
    model_rows = key_matrix.shape[0] // groups
    exact_keys, exact_values, key_total = vmem_call(
        dequantize_kernel,
        (shape_of(BLOCK, 256), shape_of(BLOCK, 256), shape_of(8, 256, jnp.float32)),
        (key_exponents, value_exponents, keys, values),
        in_specs=[SMEM, SMEM, VMEM, VMEM],
    )
    older_keys = onward(exact_keys, 2)
    last_total = onward(key_total, 1)


    near_sent, far_sent = pl.pallas_call(
        cut_kernel,
        out_shape=(shape_of(2 * model_rows, 256), shape_of(model_rows, 256)),
        in_specs=[SMEM, SMEM, HBM, HBM, pl.BlockSpec(memory_space=pl.ANY)],
        out_specs=(HBM,) * 2,
        scratch_shapes=[
            pltpu.VMEM((2 * model_rows, 256), jnp.bfloat16),
            pltpu.VMEM((model_rows, 256), jnp.bfloat16),
            pltpu.SemaphoreType.DMA((4,)),
            pltpu.SemaphoreType.DMA((2,)),
        ],
        cost_estimate=pl.CostEstimate(flops=1, bytes_accessed=1, transcendentals=0),
        compiler_params=pltpu.CompilerParams(vmem_limit_bytes=CUT_LIMIT * MEBI),
    )(place, group, key_matrix, value_matrix, keys)
    near_pairs = [
        (at * groups + there, at * groups + (there + (1 if at % 2 == 0 else groups - 1)) % groups)
        for at in range(count)
        for there in range(groups)
    ]
    older_values = onward(exact_values, 2)
    smooth = vmem_call(
        smooth_kernel, shape_of(BLOCK, 256), (place, exact_keys, older_keys, last_total), in_specs=[SMEM, VMEM, VMEM, VMEM]
    )
    older_smooth = onward(smooth, 2)
    near = lax.ppermute(near_sent, ("seq", "head"), near_pairs)

    last = to_sibling(
        jnp.where(
            core == 0,
            jnp.concatenate([smooth, exact_values], axis=1),
            jnp.concatenate([older_smooth, older_values], axis=1),
        )
    )

    queries, output_gradient, grad_cols = vmem_call(
        prepare_kernel,
        (shape_of(BLOCK, 512), shape_of(BLOCK, 512), shape_of(512, BLOCK, jnp.float32)),
        (queries, output_gradient, smooth),
        in_specs=[VMEM, VMEM, pl.BlockSpec(memory_space=pl.ANY)],
    )

    queries, near, _ = lax.optimization_barrier((queries, near, smooth))
    query_grads, gathered = [], []
    for head in range(2):
        if head == 1:
            queries, _, other_near = lax.optimization_barrier((queries, back, other_near))
        query_part, grad2, grad1, grad0 = attend_call(
            head, place, queries, output_gradient, grad_cols, older_smooth, last, smooth, older_values, exact_values
        )
        query_grads.append(query_part)
        if head == 0:
            far = along_head(lax.optimization_barrier((far_sent, grad1))[0], 2)
        sibling_grad = to_sibling(grad1)
        if head == 1:
            grad2, _ = lax.optimization_barrier((grad2, gathered[0][0]))
        back = vmem_call(merge_kernel, shape_of(BLOCK, 256), (place, grad2, sibling_grad), in_specs=[SMEM, VMEM, VMEM])
        if head == 0:
            back, near_now = lax.optimization_barrier((back, near))
            other_near = to_sibling(near_now)
        later_grad = onward(back, -2)
        scaled = vmem_call(
            functools.partial(finish_kernel, head),
            shape_of(BLOCK, 256),
            (place, key_exponents, value_exponents, grad0, sibling_grad, later_grad),
            in_specs=[SMEM, SMEM, SMEM, VMEM, VMEM, VMEM],
        )
        arrived = [scaled]
        for steps in (1, 2, 3):
            arrived.append(along_head(scaled, steps))
        gathered.append(arrived)
    far, _ = lax.optimization_barrier((far, back))
    fetched = (near, other_near, far, to_sibling(far))
    early = vmem_call(
        early_kernel,
        shape_of(model_rows, BLOCK, jnp.float32),
        (place, group, key_matrix, value_matrix, gathered[0][0], gathered[1][0], *gathered[0][1:], *fetched),
        in_specs=[SMEM, SMEM, HBM, HBM] + [VMEM] * 9,
        scratch=[pltpu.VMEM((2, model_rows, 256), jnp.bfloat16), pltpu.SemaphoreType.DMA((2,))],
        mebibytes=18,
    )
    input_grad = vmem_call(
        late_kernel,
        shape_of(model_rows, BLOCK),
        (place, early, *gathered[1][1:], *fetched),
        in_specs=[SMEM] + [VMEM] * 8,
        mebibytes=18,
    )
    return jnp.concatenate(query_grads, axis=1), input_grad


def solution(mesh):
    in_specs = (
        P("seq", "head"),
        P("seq", "head"),
        P("seq", "head"),
        P("seq", "head"),
        P("seq", "head"),
        P("seq", "head"),
        P(None, "head"),
        P(None, "head"),
    )
    out_specs = (P("seq", "head"), P("head", "seq"))
    return jax.shard_map(local, mesh=mesh, in_specs=in_specs, out_specs=out_specs, check_vma=False)
```

```python
import functools

import jax
import jax.numpy as jnp
from jax import lax
from jax.experimental import pallas as pl
from jax.experimental.pallas import tpu as pltpu
from jax.sharding import PartitionSpec as P

HEAD_SIZE = 128
QUERY_SCALE = 168
ATTEND_WINDOW = 1024
SCALE_BLOCK = 128
TILE = 256
BLOCK = 512
WINDOW_ROWS = 3 * BLOCK
HALF_ROWS = 672
LOG2_E = 1.4426950408889634
MEBI = 1024 * 1024
CUT_LIMIT = 57

NN = (((1,), (0,)), ((), ()))
NT = (((1,), (1,)), ((), ()))


def product(left, right, dims):
    return lax.dot_general(left, right, dims, preferred_element_type=jnp.float32)


def vmem_call(kernel, out_shapes, inputs, in_specs=None, scratch=(), mebibytes=8, flops=1):
    whole = pl.BlockSpec(memory_space=pltpu.VMEM)
    return pl.pallas_call(
        kernel,
        out_shape=out_shapes,
        in_specs=in_specs if in_specs is not None else [whole] * len(inputs),
        out_specs=jax.tree.map(lambda _: whole, out_shapes),
        scratch_shapes=list(scratch),
        cost_estimate=pl.CostEstimate(flops=flops, bytes_accessed=1, transcendentals=0),
        compiler_params=pltpu.CompilerParams(vmem_limit_bytes=mebibytes * MEBI),
    )(*inputs)


def shape_of(rows, columns, dtype=jnp.bfloat16):
    return jax.ShapeDtypeStruct((rows, columns), dtype)


SMEM = pl.BlockSpec(memory_space=pltpu.SMEM)
VMEM = pl.BlockSpec(memory_space=pltpu.VMEM)
HBM = pl.BlockSpec(memory_space=pltpu.MemorySpace.HBM)


def factor_of(exponent):
    return jnp.where(exponent > 0, 2.0, jnp.where(exponent < 0, 0.5, 1.0)).astype(jnp.float32)


def identity():
    row = lax.broadcasted_iota(jnp.int32, (HEAD_SIZE, HEAD_SIZE), 0)
    column = lax.broadcasted_iota(jnp.int32, (HEAD_SIZE, HEAD_SIZE), 1)
    return (row == column).astype(jnp.float32).astype(jnp.bfloat16)


def dequantize_kernel(key_exps, value_exps, keys, values, key_out, value_out, total_out):
    for part, (source, exponents, target) in enumerate(((keys, key_exps, key_out), (values, value_exps, value_out))):
        for head in range(2):
            lanes = slice(head * HEAD_SIZE, (head + 1) * HEAD_SIZE)
            total = jnp.zeros((1, HEAD_SIZE), jnp.float32)
            for block in range(BLOCK // SCALE_BLOCK):
                rows = slice(block * SCALE_BLOCK, (block + 1) * SCALE_BLOCK)
                scaled = source[rows, lanes].astype(jnp.float32) * factor_of(exponents[head, block])
                target[rows, lanes] = scaled.astype(jnp.bfloat16)
                if part == 0:
                    total = total + jnp.sum(scaled, axis=0, keepdims=True)
            if part == 0:
                total_out[:, lanes] = jnp.broadcast_to(total, (8, HEAD_SIZE))


def cut_kernel(index, group, key_matrix, value_matrix, ready, sent, rows, arrivals, departures):
    half = HALF_ROWS
    core = index[0] & 1
    near_begin = pl.multiple_of(((group[0] + 1 + 2 * core) & 3) * (2 * half), 16)
    far_begin = pl.multiple_of(((group[0] + 2) & 3) * (2 * half) + core * half, 16)
    incoming, outgoing = [], []
    first = 0
    for begin, count in ((near_begin, 2 * half), (far_begin, half)):
        for matrix in (key_matrix, value_matrix):
            at, there = len(incoming), pl.ds(first, count)
            incoming.append(pltpu.make_async_copy(matrix.at[pl.ds(begin, count), :], rows.at[there, :], arrivals.at[at]))
            outgoing.append(pltpu.make_async_copy(rows.at[there, :], sent.at[there, :], departures.at[at]))
            first += count
    for copy in incoming:
        copy.start()
    for arrived, leaving in zip(incoming, outgoing):
        arrived.wait()
        leaving.start()
    for copy in outgoing:
        copy.wait()


def smooth_kernel(place, own, older, total, smooth_out):
    first = place[0] * BLOCK
    row = lax.broadcasted_iota(jnp.int32, (BLOCK, BLOCK), 0)
    column = lax.broadcasted_iota(jnp.int32, (BLOCK, BLOCK), 1)
    upto = (column <= row).astype(jnp.float32).astype(jnp.bfloat16)
    after = (column > row).astype(jnp.float32).astype(jnp.bfloat16)
    sums = product(upto, own[...], NN) + product(after, older[...], NN) + total[0:1, :]
    position = first + lax.broadcasted_iota(jnp.int32, (BLOCK, 1), 0)
    counts = jnp.minimum(position + 1, ATTEND_WINDOW).astype(jnp.float32)
    smooth_out[...] = (own[...].astype(jnp.float32) - sums / counts).astype(jnp.bfloat16)


def attend_kernel(
    head, place, queries, grads, all_grad_cols, keys2, last, keys0, values2, values0,
    query_grad, grad2, grad1, grad0,
    key_rows, value_rows, key_cols, value_cols, weights, shares_out, score_out,
):
    scale = QUERY_SCALE ** (-0.5)
    index = place[0]
    lanes = slice(head * HEAD_SIZE, (head + 1) * HEAD_SIZE)
    last_lanes = slice(256 + head * HEAD_SIZE, 256 + (head + 1) * HEAD_SIZE)
    for at, source in enumerate((keys2, last, keys0)):
        key_rows[at * BLOCK : (at + 1) * BLOCK, :] = source[:, lanes]
    for at, source in enumerate((values2, last, values0)):
        value_rows[at * BLOCK : (at + 1) * BLOCK, :] = source[:, last_lanes if at == 1 else lanes]
    eye = identity()
    key_cols[...] = product(eye, key_rows[...], NT).astype(jnp.bfloat16)
    value_cols[...] = product(eye, value_rows[...], NT).astype(jnp.bfloat16)
    key_at = lax.broadcasted_iota(jnp.int32, (TILE, TILE), 0)
    query_at = lax.broadcasted_iota(jnp.int32, (TILE, TILE), 1)
    lowest = -jnp.inf

    valid = [index >= 2, index >= 2, index >= 1, index >= 1, None, None]
    factor = scale * LOG2_E
    parts = []
    for tile in range(BLOCK // TILE):
        for member in range(2):
            part = 2 * member + tile
            rows = slice(tile * TILE, (tile + 1) * TILE)
            columns = slice((2 * head + member) * HEAD_SIZE, (2 * head + member + 1) * HEAD_SIZE)
            parts.append(dict(
                part=part, tile=tile, member=member, rows=rows, columns=columns,
                highest=jnp.full((1, TILE), lowest, jnp.float32),
                total=jnp.zeros((1, TILE), jnp.float32),
                attended=jnp.zeros((HEAD_SIZE, TILE), jnp.float32),
                query_part=jnp.zeros((HEAD_SIZE, TILE), jnp.float32),
            ))

    def take_scores(now, step):
        source, part = now["tile"] + step, now["part"]
        scores = product(key_rows[source * TILE : (source + 1) * TILE, :], queries[now["rows"], now["columns"]], NT)
        if step == 0:
            scores = jnp.where(key_at > query_at, scores, lowest)
        if step == 4:
            scores = jnp.where(key_at <= query_at, scores, lowest)
        weights[part, step * TILE : (step + 1) * TILE, :] = scores
        peak = jnp.max(scores, axis=0, keepdims=True)
        if valid[source] is not None:
            peak = jnp.where(valid[source], peak, lowest)
        now["highest"] = jnp.maximum(now["highest"], peak)

    def take_weights(now, step):
        source, part = now["tile"] + step, now["part"]
        at = slice(step * TILE, (step + 1) * TILE)
        shift = now["highest"] * factor
        off = shift if valid[source] is None else jnp.where(valid[source], shift, jnp.inf)
        weight = jnp.exp2(weights[part, at, :] * factor - off)
        weights[part, at, :] = weight
        now["total"] = now["total"] + jnp.sum(weight, axis=0, keepdims=True)

    def take_shares(now, step):
        source, part = now["tile"] + step, now["part"]
        if step == 0:
            now["inverse"] = 1.0 / now["total"]
        rounded = (weights[part, step * TILE : (step + 1) * TILE, :] * now["inverse"]).astype(jnp.bfloat16)
        shares_out[source * TILE : (source + 1) * TILE, part * TILE : (part + 1) * TILE] = rounded
        if step == 4:
            span = slice(now["tile"] * TILE, (now["tile"] + 5) * TILE)
            now["attended"] = product(value_cols[:, span], shares_out[span, part * TILE : (part + 1) * TILE], NN)

    def take_grads(now, step):
        source, part = now["tile"] + step, now["part"]
        if step == 0:
            now["row_dot"] = jnp.sum(now["attended"] * all_grad_cols[now["columns"], now["rows"]], axis=0, keepdims=True)
        share_grad = product(value_rows[source * TILE : (source + 1) * TILE, :], grads[now["rows"], now["columns"]], NT)
        share = weights[part, step * TILE : (step + 1) * TILE, :] * now["inverse"]
        score_grad = (share * (share_grad - now["row_dot"])).astype(jnp.bfloat16)
        score_out[source * TILE : (source + 1) * TILE, part * TILE : (part + 1) * TILE] = score_grad
        if step == 4:
            span = slice(now["tile"] * TILE, (now["tile"] + 5) * TILE)
            now["query_part"] = product(key_cols[:, span], score_out[span, part * TILE : (part + 1) * TILE], NN)
            query_grad[now["rows"], now["member"] * HEAD_SIZE : (now["member"] + 1) * HEAD_SIZE] = (
                (now["query_part"] * scale).T.astype(jnp.bfloat16)
            )

    stages = (take_grads, take_shares, take_weights, take_scores)
    for turn in range(len(parts) + len(stages) - 1):
        for step in range(5):
            for stage, take in enumerate(stages):
                at = turn - (len(stages) - 1 - stage)
                if 0 <= at < len(parts):
                    take(parts[at], step)

    for source in range(6):
        rows = slice(source * TILE, (source + 1) * TILE)
        out, first = ((grad2, 0), (grad1, 2), (grad0, 4))[source // 2]
        target = slice((source - first) * TILE, (source - first + 1) * TILE)
        lanes_of = [slice((2 * head + member) * HEAD_SIZE, (2 * head + member + 1) * HEAD_SIZE) for member in range(2)]
        if 1 <= source <= 4:
            query_rows = slice(0, BLOCK)
            left = (score_out[rows, :], shares_out[rows, :])
        else:
            tile = 0 if source == 0 else 1
            query_rows = slice(tile * TILE, (tile + 1) * TILE)
            left = [
                jnp.concatenate([kept[rows, (2 * member + tile) * TILE : (2 * member + tile + 1) * TILE] for member in range(2)], axis=1)
                for kept in (score_out, shares_out)
            ]
        key_part = product(left[0], jnp.concatenate([queries[query_rows, lanes] for lanes in lanes_of], axis=0), NN)
        value_part = product(left[1], jnp.concatenate([grads[query_rows, lanes] for lanes in lanes_of], axis=0), NN)
        out[target, 0:HEAD_SIZE] = (key_part * scale).astype(out.dtype)
        out[target, HEAD_SIZE : 2 * HEAD_SIZE] = value_part.astype(out.dtype)


def attend_call(head, *operands):
    return vmem_call(
        functools.partial(attend_kernel, head),
        (shape_of(BLOCK, 256), shape_of(BLOCK, 256, jnp.float32), shape_of(BLOCK, 256), shape_of(BLOCK, 256, jnp.float32)),
        operands,
        in_specs=[SMEM] + [VMEM] * 8,
        mebibytes=18,
        scratch=[
            pltpu.VMEM((WINDOW_ROWS, HEAD_SIZE), jnp.bfloat16),
            pltpu.VMEM((WINDOW_ROWS, HEAD_SIZE), jnp.bfloat16),
            pltpu.VMEM((HEAD_SIZE, WINDOW_ROWS), jnp.bfloat16),
            pltpu.VMEM((HEAD_SIZE, WINDOW_ROWS), jnp.bfloat16),
            pltpu.VMEM((4, 5 * TILE, TILE), jnp.float32),
            pltpu.VMEM((WINDOW_ROWS, 4 * TILE), jnp.bfloat16),
            pltpu.VMEM((WINDOW_ROWS, 4 * TILE), jnp.bfloat16),
        ],
    )


def merge_kernel(place, older, arrived, out):
    odd = (place[0] & 1).astype(jnp.float32)
    out[...] = (older[...] + odd * arrived[...].astype(jnp.float32)).astype(jnp.bfloat16)


def finish_kernel(head, place, key_exps, value_exps, own, sibling, later, out):
    even = (1 - (place[0] & 1)).astype(jnp.float32)
    for block in range(BLOCK // SCALE_BLOCK):
        rows = slice(block * SCALE_BLOCK, (block + 1) * SCALE_BLOCK)
        for part, exponents in ((0, key_exps), (1, value_exps)):
            at = (rows, slice(part * HEAD_SIZE, (part + 1) * HEAD_SIZE))
            total = own[at] + even * sibling[at].astype(jnp.float32) + later[at].astype(jnp.float32)
            out[at] = (total * factor_of(exponents[head, block])).astype(jnp.bfloat16)


def remote_parts(place, head, pieces, matrices):
    before, opposite, after = pieces
    near, other_near, far, other_far = matrices
    half = HALF_ROWS
    core = place[0] & 1
    even = jnp.broadcast_to(core == 0, before.shape)
    lanes = slice(head * HEAD_SIZE, (head + 1) * HEAD_SIZE)
    first, second = before[...].astype(jnp.float32), after[...].astype(jnp.float32)
    channels = jnp.concatenate(
        [
            jnp.where(even, first, second).astype(jnp.bfloat16),
            jnp.where(even, second, first).astype(jnp.bfloat16),
            opposite[...],
        ],
        axis=1,
    )
    for at, opposite_rows in ((core, far), (1 - core, other_far)):
        begin = pl.multiple_of(at * half, 16)
        parts = []
        for matrix in (near, other_near):
            for part in range(2):
                parts.append(matrix[pl.ds(pl.multiple_of(part * 2 * half + begin, 16), half), lanes])
        parts += [opposite_rows[0:half, lanes], opposite_rows[half : 2 * half, lanes]]
        yield pl.ds(begin, half), product(jnp.concatenate(parts, axis=1), channels, NT)


def early_kernel(place, group, keys, values, own0, own1, *rest):
    pieces, matrices, out, rows, arrivals = rest[:3], rest[3:7], rest[7], rest[8], rest[9]
    begin = pl.multiple_of(group[0] * (2 * HALF_ROWS), 16)
    copies = [
        pltpu.make_async_copy(matrix.at[pl.ds(begin, 2 * HALF_ROWS), :], rows.at[part], arrivals.at[part])
        for part, matrix in enumerate((keys, values))
    ]
    for copy in copies:
        copy.start()
    for at, part in remote_parts(place, 0, pieces, matrices):
        out[at, :] = part
    for copy in copies:
        copy.wait()
    channels = jnp.concatenate(
        [own0[:, :HEAD_SIZE], own1[:, :HEAD_SIZE], own0[:, HEAD_SIZE:], own1[:, HEAD_SIZE:]], axis=1
    )
    for half_at in range(2):
        at = slice(half_at * HALF_ROWS, (half_at + 1) * HALF_ROWS)
        out[at, :] += product(jnp.concatenate([rows[0, at, :], rows[1, at, :]], axis=1), channels, NT)


def late_kernel(place, early, *rest):
    pieces, matrices, out = rest[:3], rest[3:7], rest[7]
    for at, part in remote_parts(place, 1, pieces, matrices):
        out[at, :] = (early[at, :] + part).astype(out.dtype)


def prepare_kernel(queries, grads, ready, query_out, grad_out, grad_cols):
    query_out[...] = queries[...]
    grad_out[...] = grads[...]
    eye = identity()
    for head in range(4):
        lanes = slice(head * HEAD_SIZE, (head + 1) * HEAD_SIZE)
        grad_cols[lanes, :] = product(eye, grads[:, lanes], NT)


def shift_pairs(count, steps):
    return [(at, at + steps) for at in range(max(0, -steps), min(count, count - steps))]


def local(
    queries, keys, values, output_gradient, key_exponents, value_exponents, key_matrix, value_matrix
):
    count = lax.axis_size("seq")
    groups = lax.axis_size("head")
    index = lax.axis_index("seq")
    place = index.astype(jnp.int32).reshape(1)
    group = lax.axis_index("head").astype(jnp.int32).reshape(1)
    core = index & 1
    siblings = [(at, at ^ 1) for at in range(count)]

    def to_sibling(value):
        return lax.ppermute(value, "seq", siblings)

    def onward(value, steps):
        return lax.ppermute(value, "seq", shift_pairs(count, steps))

    def along_head(value, steps):
        return lax.ppermute(value, "head", [(at, (at + steps) % groups) for at in range(groups)])

    key_exponents, value_exponents = key_exponents.T, value_exponents.T
    model_rows = key_matrix.shape[0] // groups
    exact_keys, exact_values, key_total = vmem_call(
        dequantize_kernel,
        (shape_of(BLOCK, 256), shape_of(BLOCK, 256), shape_of(8, 256, jnp.float32)),
        (key_exponents, value_exponents, keys, values),
        in_specs=[SMEM, SMEM, VMEM, VMEM],
    )
    older_keys = onward(exact_keys, 2)
    last_total = onward(key_total, 1)


    near_sent = pl.pallas_call(
        cut_kernel,
        out_shape=shape_of(3 * model_rows, 256),
        in_specs=[SMEM, SMEM, HBM, HBM, pl.BlockSpec(memory_space=pl.ANY)],
        out_specs=HBM,
        scratch_shapes=[
            pltpu.VMEM((3 * model_rows, 256), jnp.bfloat16),
            pltpu.SemaphoreType.DMA((4,)),
            pltpu.SemaphoreType.DMA((4,)),
        ],
        cost_estimate=pl.CostEstimate(flops=1, bytes_accessed=1, transcendentals=0),
        compiler_params=pltpu.CompilerParams(vmem_limit_bytes=CUT_LIMIT * MEBI),
    )(place, group, key_matrix, value_matrix, keys)
    near_pairs = [
        (at * groups + there, at * groups + (there + (1 if at % 2 == 0 else groups - 1)) % groups)
        for at in range(count)
        for there in range(groups)
    ]
    older_values = onward(exact_values, 2)
    smooth = vmem_call(
        smooth_kernel, shape_of(BLOCK, 256), (place, exact_keys, older_keys, last_total), in_specs=[SMEM, VMEM, VMEM, VMEM]
    )
    older_smooth = onward(smooth, 2)
    near = lax.ppermute(near_sent, ("seq", "head"), near_pairs)

    last = to_sibling(
        jnp.where(
            core == 0,
            jnp.concatenate([smooth, exact_values], axis=1),
            jnp.concatenate([older_smooth, older_values], axis=1),
        )
    )

    queries, output_gradient, grad_cols = vmem_call(
        prepare_kernel,
        (shape_of(BLOCK, 512), shape_of(BLOCK, 512), shape_of(512, BLOCK, jnp.float32)),
        (queries, output_gradient, smooth),
        in_specs=[VMEM, VMEM, pl.BlockSpec(memory_space=pl.ANY)],
    )

    queries, near, _ = lax.optimization_barrier((queries, near, smooth))
    query_grads, gathered = [], []
    for head in range(2):
        if head == 1:
            queries, _, other_near = lax.optimization_barrier((queries, back, other_near))
        query_part, grad2, grad1, grad0 = attend_call(
            head, place, queries, output_gradient, grad_cols, older_smooth, last, smooth, older_values, exact_values
        )
        query_grads.append(query_part)
        if head == 0:
            passed_on, _ = lax.optimization_barrier((near, grad1))
            far = lax.ppermute(passed_on[2 * model_rows :], ("seq", "head"), near_pairs)
        sibling_grad = to_sibling(grad1)
        if head == 1:
            grad2, _ = lax.optimization_barrier((grad2, gathered[0][0]))
        back = vmem_call(merge_kernel, shape_of(BLOCK, 256), (place, grad2, sibling_grad), in_specs=[SMEM, VMEM, VMEM])
        if head == 0:
            back, near_now = lax.optimization_barrier((back, near))
            other_near = to_sibling(near_now)
        later_grad = onward(back, -2)
        scaled = vmem_call(
            functools.partial(finish_kernel, head),
            shape_of(BLOCK, 256),
            (place, key_exponents, value_exponents, grad0, sibling_grad, later_grad),
            in_specs=[SMEM, SMEM, SMEM, VMEM, VMEM, VMEM],
        )
        arrived = [scaled]
        for steps in (1, 2, 3):
            arrived.append(along_head(scaled, steps))
        gathered.append(arrived)
    far, _ = lax.optimization_barrier((far, back))
    fetched = (near, other_near, far, to_sibling(far))
    early = vmem_call(
        early_kernel,
        shape_of(model_rows, BLOCK, jnp.float32),
        (place, group, key_matrix, value_matrix, gathered[0][0], gathered[1][0], *gathered[0][1:], *fetched),
        in_specs=[SMEM, SMEM, HBM, HBM] + [VMEM] * 9,
        scratch=[pltpu.VMEM((2, model_rows, 256), jnp.bfloat16), pltpu.SemaphoreType.DMA((2,))],
        mebibytes=18,
    )
    input_grad = vmem_call(
        late_kernel,
        shape_of(model_rows, BLOCK),
        (place, early, *gathered[1][1:], *fetched),
        in_specs=[SMEM] + [VMEM] * 8,
        mebibytes=18,
    )
    return jnp.concatenate(query_grads, axis=1), input_grad


def solution(mesh):
    in_specs = (
        P("seq", "head"),
        P("seq", "head"),
        P("seq", "head"),
        P("seq", "head"),
        P("seq", "head"),
        P("seq", "head"),
        P(None, "head"),
        P(None, "head"),
    )
    out_specs = (P("seq", "head"), P("head", "seq"))
    return jax.shard_map(local, mesh=mesh, in_specs=in_specs, out_specs=out_specs, check_vma=False)
```

```python
import functools

import jax
import jax.numpy as jnp
from jax import lax
from jax.experimental import pallas as pl
from jax.experimental.pallas import tpu as pltpu
from jax.sharding import PartitionSpec as P

HEAD_SIZE = 128
QUERY_SCALE = 168
ATTEND_WINDOW = 1024
SCALE_BLOCK = 128
TILE = 256
BLOCK = 512
WINDOW_ROWS = 3 * BLOCK
HALF_ROWS = 672
LOG2_E = 1.4426950408889634
MEBI = 1024 * 1024
CUT_LIMIT = 57

NN = (((1,), (0,)), ((), ()))
NT = (((1,), (1,)), ((), ()))


def product(left, right, dims):
    return lax.dot_general(left, right, dims, preferred_element_type=jnp.float32)


def vmem_call(kernel, out_shapes, inputs, in_specs=None, scratch=(), mebibytes=8, flops=1):
    whole = pl.BlockSpec(memory_space=pltpu.VMEM)
    return pl.pallas_call(
        kernel,
        out_shape=out_shapes,
        in_specs=in_specs if in_specs is not None else [whole] * len(inputs),
        out_specs=jax.tree.map(lambda _: whole, out_shapes),
        scratch_shapes=list(scratch),
        cost_estimate=pl.CostEstimate(flops=flops, bytes_accessed=1, transcendentals=0),
        compiler_params=pltpu.CompilerParams(vmem_limit_bytes=mebibytes * MEBI),
    )(*inputs)


def shape_of(rows, columns, dtype=jnp.bfloat16):
    return jax.ShapeDtypeStruct((rows, columns), dtype)


SMEM = pl.BlockSpec(memory_space=pltpu.SMEM)
VMEM = pl.BlockSpec(memory_space=pltpu.VMEM)
HBM = pl.BlockSpec(memory_space=pltpu.MemorySpace.HBM)


def factor_of(exponent):
    return jnp.where(exponent > 0, 2.0, jnp.where(exponent < 0, 0.5, 1.0)).astype(jnp.float32)


def identity():
    row = lax.broadcasted_iota(jnp.int32, (HEAD_SIZE, HEAD_SIZE), 0)
    column = lax.broadcasted_iota(jnp.int32, (HEAD_SIZE, HEAD_SIZE), 1)
    return (row == column).astype(jnp.float32).astype(jnp.bfloat16)


def dequantize_kernel(key_exps, value_exps, keys, values, key_out, value_out, total_out):
    for part, (source, exponents, target) in enumerate(((keys, key_exps, key_out), (values, value_exps, value_out))):
        for head in range(2):
            lanes = slice(head * HEAD_SIZE, (head + 1) * HEAD_SIZE)
            total = jnp.zeros((1, HEAD_SIZE), jnp.float32)
            for block in range(BLOCK // SCALE_BLOCK):
                rows = slice(block * SCALE_BLOCK, (block + 1) * SCALE_BLOCK)
                scaled = source[rows, lanes].astype(jnp.float32) * factor_of(exponents[head, block])
                target[rows, lanes] = scaled.astype(jnp.bfloat16)
                if part == 0:
                    total = total + jnp.sum(scaled, axis=0, keepdims=True)
            if part == 0:
                total_out[:, lanes] = jnp.broadcast_to(total, (8, HEAD_SIZE))


def cut_kernel(index, group, key_matrix, value_matrix, ready, sent, rows, arrivals, departures):
    half = HALF_ROWS
    core = index[0] & 1
    near_begin = pl.multiple_of(((group[0] + 1 + 2 * core) & 3) * (2 * half), 16)
    far_begin = pl.multiple_of(((group[0] + 2) & 3) * (2 * half) + core * half, 16)
    incoming, outgoing = [], []
    first = 0
    for begin, count in ((near_begin, 2 * half), (far_begin, half)):
        for matrix in (key_matrix, value_matrix):
            at, there = len(incoming), pl.ds(first, count)
            incoming.append(pltpu.make_async_copy(matrix.at[pl.ds(begin, count), :], rows.at[there, :], arrivals.at[at]))
            outgoing.append(pltpu.make_async_copy(rows.at[there, :], sent.at[there, :], departures.at[at]))
            first += count
    for copy in incoming:
        copy.start()
    for arrived, leaving in zip(incoming, outgoing):
        arrived.wait()
        leaving.start()
    for copy in outgoing:
        copy.wait()


def smooth_kernel(place, own, older, total, smooth_out):
    first = place[0] * BLOCK
    row = lax.broadcasted_iota(jnp.int32, (BLOCK, BLOCK), 0)
    column = lax.broadcasted_iota(jnp.int32, (BLOCK, BLOCK), 1)
    upto = (column <= row).astype(jnp.float32).astype(jnp.bfloat16)
    after = (column > row).astype(jnp.float32).astype(jnp.bfloat16)
    sums = product(upto, own[...], NN) + product(after, older[...], NN) + total[0:1, :]
    position = first + lax.broadcasted_iota(jnp.int32, (BLOCK, 1), 0)
    counts = jnp.minimum(position + 1, ATTEND_WINDOW).astype(jnp.float32)
    smooth_out[...] = (own[...].astype(jnp.float32) - sums / counts).astype(jnp.bfloat16)


def attend_kernel(
    head, place, queries, grads, all_grad_cols, keys2, last, keys0, values2, values0,
    query_grad, grad2, grad1, grad0,
    key_rows, value_rows, key_cols, value_cols, weights, shares_out, score_out,
):
    scale = QUERY_SCALE ** (-0.5)
    index = place[0]
    lanes = slice(head * HEAD_SIZE, (head + 1) * HEAD_SIZE)
    last_lanes = slice(256 + head * HEAD_SIZE, 256 + (head + 1) * HEAD_SIZE)
    for at, source in enumerate((keys2, last, keys0)):
        key_rows[at * BLOCK : (at + 1) * BLOCK, :] = source[:, lanes]
    for at, source in enumerate((values2, last, values0)):
        value_rows[at * BLOCK : (at + 1) * BLOCK, :] = source[:, last_lanes if at == 1 else lanes]
    eye = identity()
    key_cols[...] = product(eye, key_rows[...], NT).astype(jnp.bfloat16)
    value_cols[...] = product(eye, value_rows[...], NT).astype(jnp.bfloat16)
    key_at = lax.broadcasted_iota(jnp.int32, (TILE, TILE), 0)
    query_at = lax.broadcasted_iota(jnp.int32, (TILE, TILE), 1)
    lowest = -jnp.inf

    valid = [index >= 2, index >= 2, index >= 1, index >= 1, None, None]
    factor = scale * LOG2_E
    parts = []
    for tile in range(BLOCK // TILE):
        for member in range(2):
            part = 2 * member + tile
            rows = slice(tile * TILE, (tile + 1) * TILE)
            columns = slice((2 * head + member) * HEAD_SIZE, (2 * head + member + 1) * HEAD_SIZE)
            parts.append(dict(
                part=part, tile=tile, member=member, rows=rows, columns=columns,
                highest=jnp.full((1, TILE), lowest, jnp.float32),
                total=jnp.zeros((1, TILE), jnp.float32),
                attended=jnp.zeros((HEAD_SIZE, TILE), jnp.float32),
                query_part=jnp.zeros((HEAD_SIZE, TILE), jnp.float32),
            ))

    def take_scores(now, step):
        source, part = now["tile"] + step, now["part"]
        scores = product(key_rows[source * TILE : (source + 1) * TILE, :], queries[now["rows"], now["columns"]], NT)
        if step == 0:
            scores = jnp.where(key_at > query_at, scores, lowest)
        if step == 4:
            scores = jnp.where(key_at <= query_at, scores, lowest)
        weights[part, step * TILE : (step + 1) * TILE, :] = scores
        peak = jnp.max(scores, axis=0, keepdims=True)
        if valid[source] is not None:
            peak = jnp.where(valid[source], peak, lowest)
        now["highest"] = jnp.maximum(now["highest"], peak)

    def take_weights(now, step):
        source, part = now["tile"] + step, now["part"]
        at = slice(step * TILE, (step + 1) * TILE)
        shift = now["highest"] * factor
        off = shift if valid[source] is None else jnp.where(valid[source], shift, jnp.inf)
        weight = jnp.exp2(weights[part, at, :] * factor - off)
        weights[part, at, :] = weight
        now["total"] = now["total"] + jnp.sum(weight, axis=0, keepdims=True)

    def take_shares(now, step):
        source, part = now["tile"] + step, now["part"]
        if step == 0:
            now["inverse"] = 1.0 / now["total"]
        rounded = (weights[part, step * TILE : (step + 1) * TILE, :] * now["inverse"]).astype(jnp.bfloat16)
        shares_out[source * TILE : (source + 1) * TILE, part * TILE : (part + 1) * TILE] = rounded
        if step == 4:
            span = slice(now["tile"] * TILE, (now["tile"] + 5) * TILE)
            now["attended"] = product(value_cols[:, span], shares_out[span, part * TILE : (part + 1) * TILE], NN)

    def take_grads(now, step):
        source, part = now["tile"] + step, now["part"]
        if step == 0:
            now["row_dot"] = jnp.sum(now["attended"] * all_grad_cols[now["columns"], now["rows"]], axis=0, keepdims=True)
        share_grad = product(value_rows[source * TILE : (source + 1) * TILE, :], grads[now["rows"], now["columns"]], NT)
        share = weights[part, step * TILE : (step + 1) * TILE, :] * now["inverse"]
        score_grad = (share * (share_grad - now["row_dot"])).astype(jnp.bfloat16)
        score_out[source * TILE : (source + 1) * TILE, part * TILE : (part + 1) * TILE] = score_grad
        if step == 4:
            span = slice(now["tile"] * TILE, (now["tile"] + 5) * TILE)
            now["query_part"] = product(key_cols[:, span], score_out[span, part * TILE : (part + 1) * TILE], NN)
            query_grad[now["rows"], now["member"] * HEAD_SIZE : (now["member"] + 1) * HEAD_SIZE] = (
                (now["query_part"] * scale).T.astype(jnp.bfloat16)
            )

    stages = (take_grads, take_shares, take_weights, take_scores)
    for turn in range(len(parts) + len(stages) - 1):
        for step in range(5):
            for stage, take in enumerate(stages):
                at = turn - (len(stages) - 1 - stage)
                if 0 <= at < len(parts):
                    take(parts[at], step)

    for source in range(6):
        rows = slice(source * TILE, (source + 1) * TILE)
        out, first = ((grad2, 0), (grad1, 2), (grad0, 4))[source // 2]
        target = slice((source - first) * TILE, (source - first + 1) * TILE)
        lanes_of = [slice((2 * head + member) * HEAD_SIZE, (2 * head + member + 1) * HEAD_SIZE) for member in range(2)]
        if 1 <= source <= 4:
            query_rows = slice(0, BLOCK)
            left = (score_out[rows, :], shares_out[rows, :])
        else:
            tile = 0 if source == 0 else 1
            query_rows = slice(tile * TILE, (tile + 1) * TILE)
            left = [
                jnp.concatenate([kept[rows, (2 * member + tile) * TILE : (2 * member + tile + 1) * TILE] for member in range(2)], axis=1)
                for kept in (score_out, shares_out)
            ]
        key_part = product(left[0], jnp.concatenate([queries[query_rows, lanes] for lanes in lanes_of], axis=0), NN)
        value_part = product(left[1], jnp.concatenate([grads[query_rows, lanes] for lanes in lanes_of], axis=0), NN)
        out[target, 0:HEAD_SIZE] = (key_part * scale).astype(out.dtype)
        out[target, HEAD_SIZE : 2 * HEAD_SIZE] = value_part.astype(out.dtype)


def attend_call(head, *operands):
    return vmem_call(
        functools.partial(attend_kernel, head),
        (shape_of(BLOCK, 256), shape_of(BLOCK, 256, jnp.float32), shape_of(BLOCK, 256), shape_of(BLOCK, 256, jnp.float32)),
        operands,
        in_specs=[SMEM] + [VMEM] * 8,
        mebibytes=18,
        scratch=[
            pltpu.VMEM((WINDOW_ROWS, HEAD_SIZE), jnp.bfloat16),
            pltpu.VMEM((WINDOW_ROWS, HEAD_SIZE), jnp.bfloat16),
            pltpu.VMEM((HEAD_SIZE, WINDOW_ROWS), jnp.bfloat16),
            pltpu.VMEM((HEAD_SIZE, WINDOW_ROWS), jnp.bfloat16),
            pltpu.VMEM((4, 5 * TILE, TILE), jnp.float32),
            pltpu.VMEM((WINDOW_ROWS, 4 * TILE), jnp.bfloat16),
            pltpu.VMEM((WINDOW_ROWS, 4 * TILE), jnp.bfloat16),
        ],
    )


def merge_kernel(place, older, arrived, out):
    odd = (place[0] & 1).astype(jnp.float32)
    out[...] = (older[...] + odd * arrived[...].astype(jnp.float32)).astype(jnp.bfloat16)


def finish_kernel(head, place, key_exps, value_exps, own, sibling, later, out):
    even = (1 - (place[0] & 1)).astype(jnp.float32)
    for block in range(BLOCK // SCALE_BLOCK):
        rows = slice(block * SCALE_BLOCK, (block + 1) * SCALE_BLOCK)
        for part, exponents in ((0, key_exps), (1, value_exps)):
            at = (rows, slice(part * HEAD_SIZE, (part + 1) * HEAD_SIZE))
            total = own[at] + even * sibling[at].astype(jnp.float32) + later[at].astype(jnp.float32)
            out[at] = (total * factor_of(exponents[head, block])).astype(jnp.bfloat16)


def remote_parts(place, head, pieces, matrices):
    before, opposite, after = pieces
    near, other_near, far, other_far = matrices
    half = HALF_ROWS
    core = place[0] & 1
    even = jnp.broadcast_to(core == 0, before.shape)
    lanes = slice(head * HEAD_SIZE, (head + 1) * HEAD_SIZE)
    first, second = before[...].astype(jnp.float32), after[...].astype(jnp.float32)
    channels = jnp.concatenate(
        [
            jnp.where(even, first, second).astype(jnp.bfloat16),
            jnp.where(even, second, first).astype(jnp.bfloat16),
            opposite[...],
        ],
        axis=1,
    )
    for at, opposite_rows in ((core, far), (1 - core, other_far)):
        begin = pl.multiple_of(at * half, 16)
        parts = []
        for matrix in (near, other_near):
            for part in range(2):
                parts.append(matrix[pl.ds(pl.multiple_of(part * 2 * half + begin, 16), half), lanes])
        parts += [opposite_rows[0:half, lanes], opposite_rows[half : 2 * half, lanes]]
        yield pl.ds(begin, half), product(jnp.concatenate(parts, axis=1), channels, NT)


def early_kernel(place, group, keys, values, own0, own1, *rest):
    pieces, matrices, out, rows, arrivals = rest[:3], rest[3:7], rest[7], rest[8], rest[9]
    begin = pl.multiple_of(group[0] * (2 * HALF_ROWS), 16)
    copies = [
        pltpu.make_async_copy(matrix.at[pl.ds(begin, 2 * HALF_ROWS), :], rows.at[part], arrivals.at[part])
        for part, matrix in enumerate((keys, values))
    ]
    for copy in copies:
        copy.start()
    for at, part in remote_parts(place, 0, pieces, matrices):
        out[at, :] = part
    for copy in copies:
        copy.wait()
    channels = jnp.concatenate(
        [own0[:, :HEAD_SIZE], own1[:, :HEAD_SIZE], own0[:, HEAD_SIZE:], own1[:, HEAD_SIZE:]], axis=1
    )
    for half_at in range(2):
        at = slice(half_at * HALF_ROWS, (half_at + 1) * HALF_ROWS)
        out[at, :] += product(jnp.concatenate([rows[0, at, :], rows[1, at, :]], axis=1), channels, NT)


def late_kernel(place, early, *rest):
    pieces, matrices, out = rest[:3], rest[3:7], rest[7]
    for at, part in remote_parts(place, 1, pieces, matrices):
        out[at, :] = (early[at, :] + part).astype(out.dtype)


def prepare_kernel(queries, grads, ready, query_out, grad_out, grad_cols):
    query_out[...] = queries[...]
    grad_out[...] = grads[...]
    eye = identity()
    for head in range(4):
        lanes = slice(head * HEAD_SIZE, (head + 1) * HEAD_SIZE)
        grad_cols[lanes, :] = product(eye, grads[:, lanes], NT)


def shift_pairs(count, steps):
    return [(at, at + steps) for at in range(max(0, -steps), min(count, count - steps))]


def local(
    queries, keys, values, output_gradient, key_exponents, value_exponents, key_matrix, value_matrix
):
    count = lax.axis_size("seq")
    groups = lax.axis_size("head")
    index = lax.axis_index("seq")
    place = index.astype(jnp.int32).reshape(1)
    group = lax.axis_index("head").astype(jnp.int32).reshape(1)
    core = index & 1
    siblings = [(at, at ^ 1) for at in range(count)]

    def to_sibling(value):
        return lax.ppermute(value, "seq", siblings)

    def onward(value, steps):
        return lax.ppermute(value, "seq", shift_pairs(count, steps))

    def along_head(value, steps):
        return lax.ppermute(value, "head", [(at, (at + steps) % groups) for at in range(groups)])

    key_exponents, value_exponents = key_exponents.T, value_exponents.T
    model_rows = key_matrix.shape[0] // groups
    exact_keys, exact_values, key_total = vmem_call(
        dequantize_kernel,
        (shape_of(BLOCK, 256), shape_of(BLOCK, 256), shape_of(8, 256, jnp.float32)),
        (key_exponents, value_exponents, keys, values),
        in_specs=[SMEM, SMEM, VMEM, VMEM],
    )
    older_keys = onward(exact_keys, 2)
    last_total = onward(key_total, 1)


    near_sent = pl.pallas_call(
        cut_kernel,
        out_shape=shape_of(3 * model_rows, 256),
        in_specs=[SMEM, SMEM, HBM, HBM, pl.BlockSpec(memory_space=pl.ANY)],
        out_specs=HBM,
        scratch_shapes=[
            pltpu.VMEM((3 * model_rows, 256), jnp.bfloat16),
            pltpu.SemaphoreType.DMA((4,)),
            pltpu.SemaphoreType.DMA((4,)),
        ],
        cost_estimate=pl.CostEstimate(flops=1, bytes_accessed=1, transcendentals=0),
        compiler_params=pltpu.CompilerParams(vmem_limit_bytes=CUT_LIMIT * MEBI),
    )(place, group, key_matrix, value_matrix, keys)
    near_pairs = [
        (at * groups + there, at * groups + (there + (1 if at % 2 == 0 else groups - 1)) % groups)
        for at in range(count)
        for there in range(groups)
    ]
    older_values = onward(exact_values, 2)
    smooth = vmem_call(
        smooth_kernel, shape_of(BLOCK, 256), (place, exact_keys, older_keys, last_total), in_specs=[SMEM, VMEM, VMEM, VMEM]
    )
    older_smooth = onward(smooth, 2)
    near = lax.ppermute(near_sent, ("seq", "head"), near_pairs)

    last = to_sibling(
        jnp.where(
            core == 0,
            jnp.concatenate([smooth, exact_values], axis=1),
            jnp.concatenate([older_smooth, older_values], axis=1),
        )
    )

    queries, output_gradient, grad_cols = vmem_call(
        prepare_kernel,
        (shape_of(BLOCK, 512), shape_of(BLOCK, 512), shape_of(512, BLOCK, jnp.float32)),
        (queries, output_gradient, smooth),
        in_specs=[VMEM, VMEM, pl.BlockSpec(memory_space=pl.ANY)],
    )

    queries, near, _ = lax.optimization_barrier((queries, near, smooth))
    query_grads, gathered = [], []
    for head in range(2):
        if head == 1:
            queries, _ = lax.optimization_barrier((queries, back))
        query_part, grad2, grad1, grad0 = attend_call(
            head, place, queries, output_gradient, grad_cols, older_smooth, last, smooth, older_values, exact_values
        )
        query_grads.append(query_part)
        if head == 0:
            passed_on, _ = lax.optimization_barrier((near, grad1))
            far = lax.ppermute(passed_on[2 * model_rows :], ("seq", "head"), near_pairs)
        sibling_grad = to_sibling(grad1)
        if head == 1:
            grad2, other_near, _ = lax.optimization_barrier((grad2, other_near, gathered[0][0]))
        back = vmem_call(merge_kernel, shape_of(BLOCK, 256), (place, grad2, sibling_grad), in_specs=[SMEM, VMEM, VMEM])
        if head == 0:
            back, near_now = lax.optimization_barrier((back, near))
            other_near = to_sibling(near_now)
        later_grad = onward(back, -2)
        scaled = vmem_call(
            functools.partial(finish_kernel, head),
            shape_of(BLOCK, 256),
            (place, key_exponents, value_exponents, grad0, sibling_grad, later_grad),
            in_specs=[SMEM, SMEM, SMEM, VMEM, VMEM, VMEM],
        )
        arrived = [scaled]
        for steps in (1, 2, 3):
            arrived.append(along_head(scaled, steps))
        gathered.append(arrived)
    far, _ = lax.optimization_barrier((far, back))
    fetched = (near, other_near, far, to_sibling(far))
    early = vmem_call(
        early_kernel,
        shape_of(model_rows, BLOCK, jnp.float32),
        (place, group, key_matrix, value_matrix, gathered[0][0], gathered[1][0], *gathered[0][1:], *fetched),
        in_specs=[SMEM, SMEM, HBM, HBM] + [VMEM] * 9,
        scratch=[pltpu.VMEM((2, model_rows, 256), jnp.bfloat16), pltpu.SemaphoreType.DMA((2,))],
        mebibytes=18,
    )
    input_grad = vmem_call(
        late_kernel,
        shape_of(model_rows, BLOCK),
        (place, early, *gathered[1][1:], *fetched),
        in_specs=[SMEM] + [VMEM] * 8,
        mebibytes=18,
    )
    return jnp.concatenate(query_grads, axis=1), input_grad


def solution(mesh):
    in_specs = (
        P("seq", "head"),
        P("seq", "head"),
        P("seq", "head"),
        P("seq", "head"),
        P("seq", "head"),
        P("seq", "head"),
        P(None, "head"),
        P(None, "head"),
    )
    out_specs = (P("seq", "head"), P("head", "seq"))
    return jax.shard_map(local, mesh=mesh, in_specs=in_specs, out_specs=out_specs, check_vma=False)
```
